128 devices in a mesh: ky: 32 (over y, z_lo, x), kz: 4 (over z_hi, core).
Axes of the slice: x: 4, y: 4, z: 4 (z_hi: 2, z_lo: 2; z = z_hi * 2 + z_lo), core: 2. Of those that a mesh axis runs over, the one named last changes fastest.
Arguments:
- fields: bfloat16 [4, 2, 32, 1024, 1024], P(None, None, None, 'ky', 'kz'), may hold values from -6 to 6
- offsets: int32 [32], replicated, may hold values from 0 to 1023, as said below
Outputs:
- velocity_field: bfloat16 [3, 2, 32, 1024, 1024], P(None, None, 'ky', 'kz')
- scalar_spectrum: bfloat16 [2, 32, 1024, 1024], P(None, None, 'ky', 'kz')
The draws below stay inside these ranges and needn't reach their ends.
Inputs may be any that keep to these rules, and one draw needn't show every extreme that they name: `offsets`: ky roll of each kx plane; both ends are taken in every draw.
All inputs are finite; a program needn't handle non-finite values.
Results may differ from the reference program's by a relative error of at most 0.0059.
Values may be sent and summed in bfloat16 or wider, within the bound.
A program may use at most 128 MiB of HBM per device.

```python
import math
import jax
import jax.numpy as jnp
from jax import lax

KY = 1024
KZ = 1024
KX = 32


def draw_offsets(key, part):
    key_values, key_top, key_low = jax.random.split(key, 3)
    values = jax.random.randint(key_values, (KX,), 0, KY, dtype=jnp.int32)
    top_slot = jax.random.randint(key_top, (), 0, KX, dtype=jnp.int32)
    low_slot = (top_slot + 1 + jax.random.randint(key_low, (), 0, KX - 1, dtype=jnp.int32)) % KX
    values = values.at[top_slot].set(KY - 1)
    values = values.at[low_slot].set(0)
    return values


def level_of(rng, dims, pieces, least, largest):
    level = 1.0
    for position, parts in pieces:
        steps = jax.random.uniform(jax.random.fold_in(jax.random.fold_in(rng, 6), position), (parts,), jnp.float32, least / len(pieces), largest / len(pieces))
        level = level * jnp.repeat(jnp.exp(steps), dims[position] // parts).reshape((-1,) + (1,) * (len(dims) - 1 - position))
    return level


def scatter_about(rng, extent, scale, limit, cuts=(), held_as=jnp.bfloat16):
    result = jax.random.normal(rng, extent, jnp.float32) * scale
    if len(cuts) > 0:
        result = level_of(rng, extent, cuts, -0.22, 0.18) * result
    return jnp.clip(result, min=-limit, max=limit).astype(held_as)


def setup_inputs(seed: int = 0) -> dict:
    key_list = jax.random.split(jax.random.key(seed), 3)
    fields = scatter_about(key_list[0], (4, 2, KX, KY, KZ), 1.0, 6.0, ((3, 32), (4, 4)))
    offsets = draw_offsets(jax.random.fold_in(key_list[2], 71), 0)
    return dict(fields=fields, offsets=offsets)


def tables(length):
    counter = jnp.arange(length, dtype=jnp.int32)
    product = counter[:, None] * counter[None, :] % length
    angles = product.astype(jnp.float32) * (2.0 * math.pi / length)
    return (jnp.cos(angles).astype(jnp.bfloat16), jnp.sin(angles).astype(jnp.bfloat16))

def inverse(values, pattern, length):
    cos_table, sin_table = tables(length)

    def apply_table(operand, table):
        return jnp.einsum(pattern, operand.astype(jnp.float32), table.astype(jnp.float32), precision=lax.Precision.HIGHEST)
    real_part = values[:, 0]
    imag_part = values[:, 1]
    out_real = apply_table(real_part, cos_table) - apply_table(imag_part, sin_table)
    out_imag = apply_table(real_part, sin_table) + apply_table(imag_part, cos_table)
    factor = 1.0 / math.sqrt(length)
    return (jnp.stack([out_real, out_imag], axis=1) * factor).astype(jnp.bfloat16)

def reference(fields, offsets):
    rolled = jax.vmap(lambda kx_plane, amount: jnp.roll(kx_plane, amount, axis=2), in_axes=(2, 0), out_axes=2)(fields, offsets)

    def transform(component):
        along_y = inverse(component[None], 'cxkz,ky->cxyz', KY)
        return inverse(along_y, 'cxyk,kz->cxyz', KZ)[0]
    velocity_field = lax.map(transform, rolled[:3])
    return (velocity_field, rolled[3])
```

```python
import math

import jax
import jax.numpy as jnp
from jax import lax
from jax.sharding import PartitionSpec as P


def tables(length):
    counter = jnp.arange(length, dtype=jnp.int32)
    product = counter[:, None] * counter[None, :] % length
    angles = product.astype(jnp.float32) * (2.0 * math.pi / length)
    return (jnp.cos(angles).astype(jnp.bfloat16), jnp.sin(angles).astype(jnp.bfloat16))


def inverse(values, pattern, length):
    cos_table, sin_table = tables(length)

    def apply_table(operand, table):
        return jnp.einsum(pattern, operand, table, preferred_element_type=jnp.float32)

    real_part = values[:, 0]
    imag_part = values[:, 1]
    out_real = apply_table(real_part, cos_table) - apply_table(imag_part, sin_table)
    out_imag = apply_table(real_part, sin_table) + apply_table(imag_part, cos_table)
    factor = 1.0 / math.sqrt(length)
    return (jnp.stack([out_real, out_imag], axis=1) * factor).astype(jnp.bfloat16)


def shards(fields, offsets):
    gathered = lax.all_to_all(fields, "ky", split_axis=2, concat_axis=3, tiled=True)
    offset = lax.dynamic_slice_in_dim(offsets, lax.axis_index("ky"), 1)[0]
    count = gathered.shape[3]
    doubled = jnp.concatenate([gathered, gathered], axis=3)
    rolled = lax.dynamic_slice_in_dim(doubled, count - offset, count, axis=3)
    scalar_spectrum = lax.all_to_all(rolled[3], "ky", split_axis=2, concat_axis=1, tiled=True)
    half_done = inverse(rolled[:3], "cxkz,ky->cxyz", count)
    pieces = lax.all_to_all(half_done, "kz", split_axis=3, concat_axis=4, tiled=True)
    velocity_field = inverse(pieces, "cxyk,kz->cxyz", pieces.shape[4])
    return (velocity_field, scalar_spectrum)


def solution(mesh):
    placed = (P(None, None, None, "ky", "kz"), P())
    return jax.shard_map(
        shards,
        mesh=mesh,
        in_specs=placed,
        out_specs=(P(None, None, "ky", "kz", None), P(None, None, "ky", "kz")),
        check_vma=False,
    )
```

```python
import functools
import math

import jax
import jax.numpy as jnp
import numpy as np
from jax import lax
from jax.experimental import pallas as pl
from jax.experimental.pallas import tpu as pltpu
from jax.sharding import PartitionSpec as P

N = 1024
LOW = 32
SCALE = 1.0 / math.sqrt(N)
MESH = pl.DeviceIdType.MESH
BF16 = jnp.bfloat16
F32 = jnp.float32


def factors():
    row = np.arange(LOW, dtype=np.int64)[:, None]
    column = np.arange(N, dtype=np.int64)[None, :]
    coarse = 2.0 * np.pi / N * ((LOW * row * column) % N)
    fine = 2.0 * np.pi / N * ((row * column) % N)
    return np.stack([np.cos(coarse), np.sin(coarse), np.cos(fine), np.sin(fine)]).astype(np.float32)


def dot(a, b):
    return jnp.dot(a, b, preferred_element_type=F32)


def kernel(
    ky_count,
    kz_count,
    offsets_ref,
    fields_ref,
    factor_ref,
    velocity_ref,
    scalar_ref,
    gathered,
    rolled,
    half_done,
    across,
    result,
    turned,
    ky_cos,
    ky_sin,
    kz_cos,
    kz_sin,
    gather_send,
    gather_recv,
    own_sem,
    kz_send,
    kz_recv,
    kz_own,
    back_send,
    back_recv,
    back_own,
    out_sem,
):
    ky = lax.axis_index("ky")
    kz = lax.axis_index("kz")
    rows = N // ky_count
    part = N // kz_count

    barrier = pltpu.get_barrier_semaphore()

    @pl.loop(1, ky_count)
    def _(step):
        pl.semaphore_signal(barrier, inc=1, device_id={"ky": lax.rem(ky + step, ky_count)}, device_id_type=MESH)

    @pl.loop(1, kz_count)
    def _(step):
        pl.semaphore_signal(barrier, inc=1, device_id={"kz": lax.rem(kz + step, kz_count)}, device_id_type=MESH)

    pl.semaphore_wait(barrier, ky_count + kz_count - 2)

    my_rows = pl.ds(pl.multiple_of(ky * rows, rows), rows)
    other_rows = pl.ds(0, N - rows)

    def gather(field):
        pltpu.make_async_copy(fields_ref.at[field, :, ky], gathered.at[field, :, my_rows], own_sem.at[field]).start()

        @pl.loop(1, ky_count)
        def _(step):
            peer = lax.rem(ky + step, ky_count)
            pltpu.make_async_remote_copy(
                src_ref=fields_ref.at[field, :, peer],
                dst_ref=gathered.at[field, :, my_rows],
                send_sem=gather_send.at[field],
                recv_sem=gather_recv.at[field],
                device_id={"ky": peer},
                device_id_type=MESH,
            ).start()

    def gather_all(field):
        others = gathered.at[field, :, other_rows]
        return pltpu.make_async_remote_copy(
            src_ref=others,
            dst_ref=others,
            send_sem=gather_send.at[field],
            recv_sem=gather_recv.at[field],
            device_id={"ky": lax.rem(ky + 1, ky_count)},
            device_id_type=MESH,
        )

    def wait_gathered(field):
        pltpu.make_async_copy(fields_ref.at[field, :, ky], gathered.at[field, :, my_rows], own_sem.at[field]).wait()
        gather_all(field).wait_recv()

    for field in (3, 0, 1, 2):
        gather(field)

    offset = offsets_ref[ky]
    low_row = lax.broadcasted_iota(jnp.int32, (LOW, 1), 0)

    def turn(cos_index, sin_index, multiple, scale):
        angle = lax.rem(low_row * multiple * offset, N).astype(F32) * (2.0 * math.pi / N)
        c, s = jnp.cos(angle) * scale, jnp.sin(angle) * scale
        a, b = factor_ref[cos_index], factor_ref[sin_index]
        turned[cos_index] = a * c - b * s
        turned[sin_index] = a * s + b * c

    turn(0, 1, LOW, SCALE)
    turn(2, 3, 1, 1.0)

    def fill(source, cos_table, sin_table, scale):
        @pl.loop(0, N // LOW)
        def _(block):
            a = source[0, pl.ds(block, 1)] * scale
            b = source[1, pl.ds(block, 1)] * scale
            c, s = source[2], source[3]
            here = pl.ds(pl.multiple_of(block * LOW, LOW), LOW)
            cos_table[here] = (a * c - b * s).astype(BF16)
            sin_table[here] = (a * s + b * c).astype(BF16)

    fill(turned, ky_cos, ky_sin, 1.0)
    fill(factor_ref, kz_cos, kz_sin, SCALE)

    wait_gathered(3)

    @pl.loop(0, kz_count)
    def _(block):
        here = pl.ds(pl.multiple_of(block * part, part), part)
        target = block * part + lax.broadcasted_iota(jnp.int32, (part, N), 0)
        source = lax.rem(target + (N - offset), N)
        chosen = (lax.broadcasted_iota(jnp.int32, (part, N), 1) == source).astype(F32).astype(BF16)
        for side in range(2):
            rolled[side, here] = dot(chosen, gathered[3, side]).astype(BF16)

    def send_across(field):
        @pl.loop(1, kz_count)
        def _(step):
            peer = lax.rem(kz + step, kz_count)
            pltpu.make_async_remote_copy(
                src_ref=half_done.at[field, peer],
                dst_ref=across.at[field, :, :, pl.ds(pl.multiple_of(kz * part, part), part)],
                send_sem=kz_send.at[field],
                recv_sem=kz_recv.at[field],
                device_id={"kz": peer},
                device_id_type=MESH,
            ).start()

        own_across(field).start()

    def own_across(field):
        return pltpu.make_async_copy(
            half_done.at[field, kz],
            across.at[field, :, :, pl.ds(pl.multiple_of(kz * part, part), part)],
            kz_own.at[field],
        )

    def all_across(field):
        others = across.at[field, :, :, pl.ds(0, N - part)]
        return pltpu.make_async_remote_copy(
            src_ref=others,
            dst_ref=others,
            send_sem=kz_send.at[field],
            recv_sem=kz_recv.at[field],
            device_id={"kz": lax.rem(kz + 1, kz_count)},
            device_id_type=MESH,
        )

    for field in range(3):
        wait_gathered(field)

        @pl.loop(0, kz_count)
        def _(block):
            here = pl.ds(pl.multiple_of(block * part, part), part)
            c, s = ky_cos[here], ky_sin[here]
            real, imag = gathered[field, 0], gathered[field, 1]
            half_done[field, block, 0] = (dot(c, real) - dot(s, imag)).astype(BF16)
            half_done[field, block, 1] = (dot(s, real) + dot(c, imag)).astype(BF16)

        send_across(field)

    def own_back():
        return pltpu.make_async_copy(rolled.at[:, my_rows], scalar_ref.at[:, ky], back_own)

    @pl.loop(1, ky_count)
    def _(step):
        peer = lax.rem(ky + step, ky_count)
        pltpu.make_async_remote_copy(
            src_ref=rolled.at[:, pl.ds(pl.multiple_of(peer * rows, rows), rows)],
            dst_ref=scalar_ref.at[:, ky],
            send_sem=back_send,
            recv_sem=back_recv,
            device_id={"ky": peer},
            device_id_type=MESH,
        ).start()

    own_back().start()

    for field in range(3):
        own_across(field).wait()
        all_across(field).wait_recv()

        @pl.loop(0, kz_count)
        def _(block):
            here = pl.ds(pl.multiple_of(block * part, part), part)
            c, s = kz_cos[:, here], kz_sin[:, here]
            real, imag = across[field, 0], across[field, 1]
            result[field, 0, :, here] = (dot(real, c) - dot(imag, s)).astype(BF16)
            result[field, 1, :, here] = (dot(real, s) + dot(imag, c)).astype(BF16)

        pltpu.make_async_copy(result.at[field], velocity_ref.at[field, :, 0], out_sem.at[field]).start()

    others_back = scalar_ref.at[:, pl.ds(0, ky_count - 1)]
    back = pltpu.make_async_remote_copy(
        src_ref=others_back,
        dst_ref=others_back,
        send_sem=back_send,
        recv_sem=back_recv,
        device_id={"ky": lax.rem(ky + 1, ky_count)},
        device_id_type=MESH,
    )
    back.wait_recv()
    own_back().wait()
    for field in range(3):
        pltpu.make_async_copy(result.at[field], velocity_ref.at[field, :, 0], out_sem.at[field]).wait()
    for field in range(4):
        gather_all(field).wait_send()
    for field in range(3):
        all_across(field).wait_send()
    back.wait_send()


def shards(fields, offsets):
    ky_count, kz_count = lax.axis_size("ky"), lax.axis_size("kz")
    rows, part = fields.shape[3], fields.shape[4]
    in_vmem = lambda *shape: pltpu.VMEM(shape, BF16)
    dma = lambda *shape: pltpu.SemaphoreType.DMA(shape)
    return pl.pallas_call(
        functools.partial(kernel, ky_count, kz_count),
        out_shape=(
            jax.ShapeDtypeStruct((3, 2, 1, part, N), BF16),
            jax.ShapeDtypeStruct((2, ky_count, rows, part), BF16),
        ),
        in_specs=[
            pl.BlockSpec(memory_space=pltpu.SMEM),
            pl.BlockSpec(memory_space=pl.ANY),
            pl.BlockSpec(memory_space=pltpu.VMEM),
        ],
        out_specs=(pl.BlockSpec(memory_space=pl.ANY), pl.BlockSpec(memory_space=pl.ANY)),
        scratch_shapes=[
            in_vmem(4, 2, N, part),
            in_vmem(2, N, part),
            in_vmem(3, kz_count, 2, part, part),
            in_vmem(3, 2, part, N),
            in_vmem(3, 2, part, N),
            pltpu.VMEM((4, LOW, N), F32),
            in_vmem(N, N),
            in_vmem(N, N),
            in_vmem(N, N),
            in_vmem(N, N),
            dma(4),
            dma(4),
            dma(4),
            dma(3),
            dma(3),
            dma(3),
            pltpu.SemaphoreType.DMA,
            pltpu.SemaphoreType.DMA,
            pltpu.SemaphoreType.DMA,
            dma(3),
        ],
        compiler_params=pltpu.CompilerParams(
            collective_id=0, has_side_effects=True, vmem_limit_bytes=48 * 2**20
        ),
        name="roll_and_transform",
    )(offsets, fields, jnp.asarray(factors()))


def solution(mesh):
    placed = (P(None, None, None, "ky", "kz"), P())
    return jax.shard_map(
        shards,
        mesh=mesh,
        in_specs=placed,
        out_specs=(P(None, None, "ky", "kz", None), P(None, None, "ky", "kz")),
        check_vma=False,
    )
```

```python
import functools
import math

import jax
import jax.numpy as jnp
from jax import lax
from jax.experimental import pallas as pl
from jax.experimental.pallas import tpu as pltpu
from jax.sharding import PartitionSpec as P

N = 1024
LOW = 32
SCALE = 1.0 / math.sqrt(N)
MESH = pl.DeviceIdType.MESH
BF16 = jnp.bfloat16
F32 = jnp.float32
SCALAR = 3
PIECES = (1, 1, 4)


def dot(a, b):
    return jnp.dot(a, b, preferred_element_type=F32)


def kernel(
    ky_count,
    kz_count,
    offsets_ref,
    fields_ref,
    velocity_ref,
    scalar_ref,
    gathered,
    relay,
    rolled,
    back_relay,
    half_done,
    across,
    factor,
    turned,
    ky_cos,
    ky_sin,
    kz_cos,
    kz_sin,
    word,
    relay_send,
    relay_recv,
    relay_own,
    gather_send,
    gather_recv,
    own_sem,
    kz_send,
    kz_recv,
    kz_own,
    over_send,
    over_recv,
    back_send,
    back_recv,
    back_own,
):
    ky = lax.axis_index("ky")
    kz = lax.axis_index("kz")
    rows = N // ky_count
    part = N // kz_count
    plane_count = ky_count // 2

    x, low_z, y = lax.rem(ky, 4), lax.rem(ky // 4, 2), ky // 8

    def at(new_y, new_low_z, new_x):
        return lax.rem(new_y, 4) * 8 + new_low_z * 4 + lax.rem(new_x, 4)

    partner = at(y, 1 - low_z, x)
    beside_x = (at(y, low_z, x + 1), at(y, low_z, x + 3))
    beside_y = (at(y + 1, low_z, x), at(y + 3, low_z, x))

    def kz_peers():
        return [lax.rem(kz // 2 + step // 2, 2) * 2 + lax.rem(kz + step, 2) for step in (2, 3, 1)]

    def signal(sem, **device):
        pl.semaphore_signal(sem, inc=1, device_id=device, device_id_type=MESH)

    def remote(src, dst, send_sem, recv_sem, **device):
        return pltpu.make_async_remote_copy(
            src_ref=src, dst_ref=dst, send_sem=send_sem, recv_sem=recv_sem, device_id=device, device_id_type=MESH
        )

    barrier = pltpu.get_barrier_semaphore()
    for peer in (partner, *beside_x, *beside_y):
        signal(barrier, ky=peer)
    for peer in kz_peers():
        signal(barrier, kz=peer)
    pl.semaphore_wait(barrier, 8)

    def send_over(field):
        for group in range(4):
            remote(
                fields_ref.at[field, :, pl.ds(group * 8 + (1 - low_z) * 4, 4)],
                relay.at[field, :, pl.ds(group * 4, 4)],
                relay_send.at[field],
                relay_recv.at[field],
                ky=partner,
            ).start()

    def all_over(field):
        return remote(
            relay.at[field], relay.at[field], relay_send.at[field], relay_recv.at[field], ky=partner
        )

    for field in (SCALAR, 0, 1, 2):
        send_over(field)

    for turn_index, peers in enumerate((beside_x, beside_y, beside_y, (partner,))):
        for peer in peers:
            signal(word.at[turn_index], ky=peer)
        pl.semaphore_wait(word.at[turn_index], len(peers))

    def rows_of(block):
        return pl.ds(pl.multiple_of(block * rows, rows), rows)

    my_rows, partner_rows = rows_of(ky), rows_of(partner)

    def in_plane(step):
        number = lax.rem(mine + step, plane_count)
        return number, at(number // 4, low_z, number)

    mine = y * 4 + x

    def own_copy(field):
        return pltpu.make_async_copy(fields_ref.at[field, :, ky], gathered.at[field, :, my_rows], own_sem.at[field])

    def relay_copy(field):
        return pltpu.make_async_copy(
            relay.at[field, :, mine], gathered.at[field, :, partner_rows], relay_own.at[field]
        )

    def gather(field):
        own_copy(field).start()

        @pl.loop(1, plane_count)
        def _(step):
            _, peer = in_plane(step)
            remote(
                fields_ref.at[field, :, peer],
                gathered.at[field, :, my_rows],
                gather_send.at[field],
                gather_recv.at[field],
                ky=peer,
            ).start()

    def pass_on(field):
        all_over(field).wait_recv()
        relay_copy(field).start()

        @pl.loop(1, plane_count)
        def _(step):
            number, peer = in_plane(step)
            remote(
                relay.at[field, :, number],
                gathered.at[field, :, partner_rows],
                gather_send.at[field],
                gather_recv.at[field],
                ky=peer,
            ).start()

    def gather_all(field):
        others = gathered.at[field, :, pl.ds(0, (ky_count - 2) * rows)]
        return remote(others, others, gather_send.at[field], gather_recv.at[field], ky=partner)

    def wait_gathered(field):
        own_copy(field).wait()
        relay_copy(field).wait()
        gather_all(field).wait_recv()

    gather(SCALAR)
    gather(0)

    offset = offsets_ref[ky]
    some = LOW // 4

    @pl.loop(0, 4)
    def _(group):
        here = pl.ds(pl.multiple_of(group * some, some), some)
        row = group * some + lax.broadcasted_iota(jnp.int32, (some, N), 0)
        column = lax.broadcasted_iota(jnp.int32, (some, N), 1)
        low_row = group * some + lax.broadcasted_iota(jnp.int32, (some, 128), 0)

        def wave(turns):
            angle = lax.rem(turns, N).astype(F32) * (2.0 * math.pi / N)
            return jnp.cos(angle), jnp.sin(angle)

        for index, multiple, scale in ((0, LOW, SCALE), (2, 1, 1.0)):
            a, b = wave(row * multiple * column)
            a, b = a * scale, b * scale
            c, s = wave(low_row * multiple * offset)
            c, s = c[:, :1], s[:, :1]
            factor[index, here] = a
            factor[index + 1, here] = b
            turned[index, here] = a * c - b * s
            turned[index + 1, here] = a * s + b * c

    def fill(source, cos_table, sin_table):
        @pl.loop(0, N // LOW)
        def _(block):
            a = source[0, pl.ds(block, 1)]
            b = source[1, pl.ds(block, 1)]
            c, s = source[2], source[3]
            here = pl.ds(pl.multiple_of(block * LOW, LOW), LOW)
            cos_table[here] = (a * c - b * s).astype(BF16)
            sin_table[here] = (a * s + b * c).astype(BF16)

    fill(turned, ky_cos, ky_sin)

    pass_on(SCALAR)
    gather(1)
    fill(factor, kz_cos, kz_sin)
    pass_on(0)
    gather(2)

    wait_gathered(SCALAR)

    @pl.loop(0, kz_count)
    def _(block):
        here = pl.ds(pl.multiple_of(block * part, part), part)
        target = block * part + lax.broadcasted_iota(jnp.int32, (part, N), 0)
        source = lax.rem(target + (N - offset), N)
        chosen = (lax.broadcasted_iota(jnp.int32, (part, N), 1) == source).astype(F32).astype(BF16)
        for side in range(2):
            rolled[side, here] = dot(chosen, gathered[SCALAR, side]).astype(BF16)

    for group in range(4):
        remote(
            rolled.at[:, pl.ds(pl.multiple_of(group * 256 + (1 - low_z) * 128, 128), 128)],
            back_relay.at[:, pl.ds(group * 128, 128)],
            over_send,
            over_recv,
            ky=partner,
        ).start()

    own_back = pltpu.make_async_copy(rolled.at[:, my_rows], scalar_ref.at[:, ky], back_own.at[0])
    own_back.start()

    @pl.loop(1, plane_count)
    def _(step):
        _, peer = in_plane(step)
        remote(rolled.at[:, rows_of(peer)], scalar_ref.at[:, ky], back_send, back_recv, ky=peer).start()

    my_part = pl.ds(pl.multiple_of(kz * part, part), part)

    def piece_rows(field, piece):
        size = part // PIECES[field]
        return pl.ds(piece * size, size)

    def own_across(field, piece):
        some_rows = piece_rows(field, piece)
        return pltpu.make_async_copy(
            half_done.at[field, kz, :, some_rows], across.at[field, :, some_rows, my_part], kz_own.at[field, piece]
        )

    def all_across(field, piece):
        others = across.at[field, :, piece_rows(field, piece), pl.ds(0, N - part)]
        return remote(others, others, kz_send.at[field, piece], kz_recv.at[field, piece], kz=kz_peers()[0])

    for field in range(3):
        if field:
            pass_on(field)
        wait_gathered(field)

        @pl.loop(0, kz_count)
        def _(block):
            here = pl.ds(pl.multiple_of(block * part, part), part)
            c, s = ky_cos[here], ky_sin[here]
            real, imag = gathered[field, 0], gathered[field, 1]
            half_done[field, block, 0] = (dot(c, real) - dot(s, imag)).astype(BF16)
            half_done[field, block, 1] = (dot(s, real) + dot(c, imag)).astype(BF16)

        for piece in range(PIECES[field]):
            some_rows = piece_rows(field, piece)
            for peer in kz_peers():
                remote(
                    half_done.at[field, peer, :, some_rows],
                    across.at[field, :, some_rows, my_part],
                    kz_send.at[field, piece],
                    kz_recv.at[field, piece],
                    kz=peer,
                ).start()
            own_across(field, piece).start()

    over = remote(back_relay, back_relay, over_send, over_recv, ky=partner)
    over.wait_recv()
    relay_back = pltpu.make_async_copy(back_relay.at[:, rows_of(mine)], scalar_ref.at[:, partner], back_own.at[1])
    relay_back.start()

    @pl.loop(1, plane_count)
    def _(step):
        number, peer = in_plane(step)
        remote(back_relay.at[:, rows_of(number)], scalar_ref.at[:, partner], back_send, back_recv, ky=peer).start()

    for field in range(3):
        for piece in range(PIECES[field]):
            own_across(field, piece).wait()
            all_across(field, piece).wait_recv()
            some_rows = piece_rows(field, piece)
            size = part // PIECES[field]

            @pl.loop(0, kz_count)
            def _(block):
                here = pl.ds(pl.multiple_of(block * part, part), part)
                both = across[field, :, some_rows].reshape(2 * size, N)
                by_cos, by_sin = dot(both, kz_cos[:, here]), dot(both, kz_sin[:, here])
                velocity_ref[field, 0, 0, some_rows, here] = (by_cos[:size] - by_sin[size:]).astype(BF16)
                velocity_ref[field, 1, 0, some_rows, here] = (by_sin[:size] + by_cos[size:]).astype(BF16)

    others_back = scalar_ref.at[:, pl.ds(0, ky_count - 2)]
    back = remote(others_back, others_back, back_send, back_recv, ky=partner)
    back.wait_recv()
    own_back.wait()
    relay_back.wait()
    for field in range(4):
        all_over(field).wait_send()
        gather_all(field).wait_send()
    for field in range(3):
        for piece in range(PIECES[field]):
            all_across(field, piece).wait_send()
    over.wait_send()
    back.wait_send()


def shards(fields, offsets):
    ky_count, kz_count = lax.axis_size("ky"), lax.axis_size("kz")
    rows, part = fields.shape[3], fields.shape[4]
    in_vmem = lambda *shape: pltpu.VMEM(shape, BF16)
    dma = lambda *shape: pltpu.SemaphoreType.DMA(shape)
    most = max(PIECES)
    return pl.pallas_call(
        functools.partial(kernel, ky_count, kz_count),
        out_shape=(
            jax.ShapeDtypeStruct((3, 2, 1, part, N), BF16),
            jax.ShapeDtypeStruct((2, ky_count, rows, part), BF16),
        ),
        in_specs=[pl.BlockSpec(memory_space=pltpu.SMEM), pl.BlockSpec(memory_space=pl.ANY)],
        out_specs=(pl.BlockSpec(memory_space=pltpu.VMEM), pl.BlockSpec(memory_space=pltpu.VMEM)),
        scratch_shapes=[
            in_vmem(4, 2, N, part),
            in_vmem(4, 2, ky_count // 2, rows, part),
            in_vmem(2, N, part),
            in_vmem(2, N // 2, part),
            in_vmem(3, kz_count, 2, part, part),
            in_vmem(3, 2, part, N),
            pltpu.VMEM((4, LOW, N), F32),
            pltpu.VMEM((4, LOW, N), F32),
            in_vmem(N, N),
            in_vmem(N, N),
            in_vmem(N, N),
            in_vmem(N, N),
            pltpu.SemaphoreType.REGULAR((4,)),
            dma(4),
            dma(4),
            dma(4),
            dma(4),
            dma(4),
            dma(4),
            dma(3, most),
            dma(3, most),
            dma(3, most),
            pltpu.SemaphoreType.DMA,
            pltpu.SemaphoreType.DMA,
            pltpu.SemaphoreType.DMA,
            pltpu.SemaphoreType.DMA,
            dma(2),
        ],
        compiler_params=pltpu.CompilerParams(
            collective_id=0, has_side_effects=True, vmem_limit_bytes=48 * 2**20
        ),
        name="roll_and_transform",
    )(offsets, fields)


def solution(mesh):
    placed = (P(None, None, None, "ky", "kz"), P())
    return jax.shard_map(
        shards,
        mesh=mesh,
        in_specs=placed,
        out_specs=(P(None, None, "ky", "kz", None), P(None, None, "ky", "kz")),
        check_vma=False,
    )
```

```python
import functools
import math

import jax
import jax.numpy as jnp
from jax import lax
from jax.experimental import pallas as pl
from jax.experimental.pallas import tpu as pltpu
from jax.sharding import PartitionSpec as P

N = 1024
LOW = 32
SCALE = 1.0 / math.sqrt(N)
MESH = pl.DeviceIdType.MESH
BF16 = jnp.bfloat16
F32 = jnp.float32
SCALAR = 3
PIECES = (1, 1, 4)
LAST = (2, 3)
ROUNDS = 7


def dot(a, b):
    return jnp.dot(a, b, preferred_element_type=F32)


def along_z(half_ref, cos_ref, sin_ref, out_ref, blocks):
    size = half_ref.shape[1]
    width = N // blocks

    @pl.loop(0, blocks)
    def _(block):
        here = pl.ds(pl.multiple_of(block * width, width), width)
        both = half_ref[...].reshape(2 * size, N)
        by_cos, by_sin = dot(both, cos_ref[:, here]), dot(both, sin_ref[:, here])
        out_ref[0, :, here] = (by_cos[:size] - by_sin[size:]).astype(BF16)
        out_ref[1, :, here] = (by_sin[:size] + by_cos[size:]).astype(BF16)


def finish(blocks, velocity_ref, scalar_ref, last_ref, cos_ref, sin_ref, velocity_out, scalar_out, result, sems):
    size = last_ref.shape[1]
    done = pl.ds(0, N // blocks - size)
    copies = [
        pltpu.make_async_copy(velocity_ref.at[0:2], velocity_out.at[0:2, :, 0], sems.at[0]),
        pltpu.make_async_copy(velocity_ref.at[2, :, done], velocity_out.at[2, :, 0, done], sems.at[1]),
        pltpu.make_async_copy(scalar_ref, scalar_out, sems.at[2]),
        pltpu.make_async_copy(result, velocity_out.at[2, :, 0, pl.ds(N // blocks - size, size)], sems.at[3]),
    ]
    for copy in copies[:3]:
        copy.start()
    along_z(last_ref, cos_ref, sin_ref, result, blocks)
    copies[3].start()
    for copy in copies:
        copy.wait()


def kernel(
    ky_count,
    kz_count,
    offsets_ref,
    fields_ref,
    velocity_ref,
    scalar_ref,
    last_ref,
    kz_cos,
    kz_sin,
    gathered,
    relay,
    rolled,
    back_relay,
    half_done,
    across,
    factor,
    turned,
    ky_cos,
    ky_sin,
    word,
    relay_send,
    relay_recv,
    relay_own,
    gather_send,
    gather_recv,
    own_sem,
    kz_send,
    kz_recv,
    kz_own,
    over_send,
    over_recv,
    back_send,
    back_recv,
    back_own,
):
    ky = lax.axis_index("ky")
    kz = lax.axis_index("kz")
    rows = N // ky_count
    part = N // kz_count
    plane_count = ky_count // 2

    x, low_z, y = lax.rem(ky, 4), lax.rem(ky // 4, 2), ky // 8

    def at(new_y, new_low_z, new_x):
        return lax.rem(new_y, 4) * 8 + new_low_z * 4 + lax.rem(new_x, 4)

    partner = at(y, 1 - low_z, x)

    def each_beside_x(act):
        pl.when(x > 0)(lambda: act(at(y, low_z, x + 3)))
        pl.when(x < 3)(lambda: act(at(y, low_z, x + 1)))

    def each_beside_y(act):
        pl.when(y > 0)(lambda: act(at(y + 3, low_z, x)))
        pl.when(y < 3)(lambda: act(at(y + 1, low_z, x)))

    def count_beside(place):
        return 2 - jnp.where(place == 0, 1, 0) - jnp.where(place == 3, 1, 0)

    def kz_peers():
        return [lax.rem(kz // 2 + step // 2, 2) * 2 + lax.rem(kz + step, 2) for step in (2, 3, 1)]

    def signal(sem, **device):
        pl.semaphore_signal(sem, inc=1, device_id=device, device_id_type=MESH)

    def remote(src, dst, send_sem, recv_sem, **device):
        return pltpu.make_async_remote_copy(
            src_ref=src, dst_ref=dst, send_sem=send_sem, recv_sem=recv_sem, device_id=device, device_id_type=MESH
        )

    barrier = pltpu.get_barrier_semaphore()
    signal(barrier, ky=partner)
    each_beside_x(lambda peer: signal(barrier, ky=peer))
    each_beside_y(lambda peer: signal(barrier, ky=peer))
    for peer in kz_peers():
        signal(barrier, kz=peer)
    pl.semaphore_wait(barrier, 4 + count_beside(x) + count_beside(y))

    def send_over(field):
        for group in range(4):
            remote(
                fields_ref.at[field, :, pl.ds(group * 8 + (1 - low_z) * 4, 4)],
                relay.at[field, :, pl.ds(group * 4, 4)],
                relay_send.at[field],
                relay_recv.at[field],
                ky=partner,
            ).start()

    def all_over(field):
        return remote(
            relay.at[field], relay.at[field], relay_send.at[field], relay_recv.at[field], ky=partner
        )

    for field in (SCALAR, 0, 1, 2):
        send_over(field)

    for index in range(3):
        each_beside_x(lambda peer: signal(word.at[index], ky=peer))
        pl.semaphore_wait(word.at[index], count_beside(x))
    for index in range(3, 6):
        each_beside_y(lambda peer: signal(word.at[index], ky=peer))
        pl.semaphore_wait(word.at[index], count_beside(y))
    signal(word.at[6], ky=partner)
    pl.semaphore_wait(word.at[6], 1)

    def rows_of(block):
        return pl.ds(pl.multiple_of(block * rows, rows), rows)

    my_rows, partner_rows = rows_of(ky), rows_of(partner)

    def in_plane(step):
        number = lax.rem(mine + step, plane_count)
        return number, at(number // 4, low_z, number)

    mine = y * 4 + x

    def own_copy(field):
        return pltpu.make_async_copy(fields_ref.at[field, :, ky], gathered.at[field, :, my_rows], own_sem.at[field])

    def relay_copy(field):
        return pltpu.make_async_copy(
            relay.at[field, :, mine], gathered.at[field, :, partner_rows], relay_own.at[field]
        )

    def gather(field):
        own_copy(field).start()

        @pl.loop(1, plane_count)
        def _(step):
            _, peer = in_plane(step)
            remote(
                fields_ref.at[field, :, peer],
                gathered.at[field, :, my_rows],
                gather_send.at[field],
                gather_recv.at[field],
                ky=peer,
            ).start()

    def pass_on(field):
        all_over(field).wait_recv()
        relay_copy(field).start()

        @pl.loop(1, plane_count)
        def _(step):
            number, peer = in_plane(step)
            remote(
                relay.at[field, :, number],
                gathered.at[field, :, partner_rows],
                gather_send.at[field],
                gather_recv.at[field],
                ky=peer,
            ).start()

    def gather_all(field):
        others = gathered.at[field, :, pl.ds(0, (ky_count - 2) * rows)]
        return remote(others, others, gather_send.at[field], gather_recv.at[field], ky=partner)

    def wait_gathered(field):
        own_copy(field).wait()
        relay_copy(field).wait()
        gather_all(field).wait_recv()

    gather(SCALAR)
    gather(0)

    offset = offsets_ref[ky]
    some = LOW // 4

    @pl.loop(0, 4)
    def _(group):
        here = pl.ds(pl.multiple_of(group * some, some), some)
        row = group * some + lax.broadcasted_iota(jnp.int32, (some, N), 0)
        column = lax.broadcasted_iota(jnp.int32, (some, N), 1)
        low_row = group * some + lax.broadcasted_iota(jnp.int32, (some, 128), 0)

        def wave(turns):
            angle = lax.rem(turns, N).astype(F32) * (2.0 * math.pi / N)
            return jnp.cos(angle), jnp.sin(angle)

        for index, multiple, scale in ((0, LOW, SCALE), (2, 1, 1.0)):
            a, b = wave(row * multiple * column)
            a, b = a * scale, b * scale
            c, s = wave(low_row * multiple * offset)
            c, s = c[:, :1], s[:, :1]
            factor[index, here] = a
            factor[index + 1, here] = b
            turned[index, here] = a * c - b * s
            turned[index + 1, here] = a * s + b * c

    def fill(source, cos_table, sin_table):
        @pl.loop(0, N // LOW)
        def _(block):
            a = source[0, pl.ds(block, 1)]
            b = source[1, pl.ds(block, 1)]
            c, s = source[2], source[3]
            here = pl.ds(pl.multiple_of(block * LOW, LOW), LOW)
            cos_table[here] = (a * c - b * s).astype(BF16)
            sin_table[here] = (a * s + b * c).astype(BF16)

    fill(turned, ky_cos, ky_sin)

    pass_on(SCALAR)
    gather(1)
    fill(factor, kz_cos, kz_sin)
    pass_on(0)
    gather(2)

    wait_gathered(SCALAR)

    @pl.loop(0, kz_count)
    def _(block):
        here = pl.ds(pl.multiple_of(block * part, part), part)
        target = block * part + lax.broadcasted_iota(jnp.int32, (part, N), 0)
        source = lax.rem(target + (N - offset), N)
        chosen = (lax.broadcasted_iota(jnp.int32, (part, N), 1) == source).astype(F32).astype(BF16)
        for side in range(2):
            rolled[side, here] = dot(chosen, gathered[SCALAR, side]).astype(BF16)

    for group in range(4):
        remote(
            rolled.at[:, pl.ds(pl.multiple_of(group * 256 + (1 - low_z) * 128, 128), 128)],
            back_relay.at[:, pl.ds(group * 128, 128)],
            over_send,
            over_recv,
            ky=partner,
        ).start()

    own_back = pltpu.make_async_copy(rolled.at[:, my_rows], scalar_ref.at[:, ky], back_own.at[0])
    own_back.start()

    @pl.loop(1, plane_count)
    def _(step):
        _, peer = in_plane(step)
        remote(rolled.at[:, rows_of(peer)], scalar_ref.at[:, ky], back_send, back_recv, ky=peer).start()

    my_part = pl.ds(pl.multiple_of(kz * part, part), part)

    def piece_rows(field, piece):
        size = part // PIECES[field]
        return pl.ds(piece * size, size)

    def own_across(field, piece):
        some_rows = piece_rows(field, piece)
        return pltpu.make_async_copy(
            half_done.at[field, kz, :, some_rows], across.at[field, :, some_rows, my_part], kz_own.at[field, piece]
        )

    def all_across(field, piece):
        others = across.at[field, :, piece_rows(field, piece), pl.ds(0, N - part)]
        return remote(others, others, kz_send.at[field, piece], kz_recv.at[field, piece], kz=kz_peers()[0])

    for field in range(3):
        if field:
            pass_on(field)
        wait_gathered(field)

        @pl.loop(0, kz_count)
        def _(block):
            here = pl.ds(pl.multiple_of(block * part, part), part)
            c, s = ky_cos[here], ky_sin[here]
            real, imag = gathered[field, 0], gathered[field, 1]
            half_done[field, block, 0] = (dot(c, real) - dot(s, imag)).astype(BF16)
            half_done[field, block, 1] = (dot(s, real) + dot(c, imag)).astype(BF16)

        for piece in range(PIECES[field]):
            some_rows = piece_rows(field, piece)
            for peer in kz_peers():
                remote(
                    half_done.at[field, peer, :, some_rows],
                    across.at[field, :, some_rows, my_part],
                    kz_send.at[field, piece],
                    kz_recv.at[field, piece],
                    kz=peer,
                ).start()
            own_across(field, piece).start()

    over = remote(back_relay, back_relay, over_send, over_recv, ky=partner)
    over.wait_recv()
    relay_back = pltpu.make_async_copy(back_relay.at[:, rows_of(mine)], scalar_ref.at[:, partner], back_own.at[1])
    relay_back.start()

    @pl.loop(1, plane_count)
    def _(step):
        number, peer = in_plane(step)
        remote(back_relay.at[:, rows_of(number)], scalar_ref.at[:, partner], back_send, back_recv, ky=peer).start()

    for field in range(3):
        for piece in range(PIECES[field]):
            own_across(field, piece).wait()
            all_across(field, piece).wait_recv()
            if (field, piece) != LAST:
                some_rows = piece_rows(field, piece)
                along_z(
                    across.at[field, :, some_rows], kz_cos, kz_sin, velocity_ref.at[field, :, some_rows], kz_count
                )

    last_ref[...] = across[LAST[0], :, piece_rows(*LAST)]
    others_back = scalar_ref.at[:, pl.ds(0, ky_count - 2)]
    back = remote(others_back, others_back, back_send, back_recv, ky=partner)
    back.wait_recv()
    own_back.wait()
    relay_back.wait()
    for field in range(4):
        all_over(field).wait_send()
        gather_all(field).wait_send()
    for field in range(3):
        for piece in range(PIECES[field]):
            all_across(field, piece).wait_send()
    over.wait_send()
    back.wait_send()


def shards(fields, offsets):
    ky_count, kz_count = lax.axis_size("ky"), lax.axis_size("kz")
    rows, part = fields.shape[3], fields.shape[4]
    in_vmem = lambda *shape: pltpu.VMEM(shape, BF16)
    dma = lambda *shape: pltpu.SemaphoreType.DMA(shape)
    most = max(PIECES)
    vmem, hbm = pl.BlockSpec(memory_space=pltpu.VMEM), pl.BlockSpec(memory_space=pltpu.HBM)
    shape = lambda *dims: jax.ShapeDtypeStruct(dims, BF16)
    scalar_shape = shape(2, ky_count, rows, part)
    piece = part // PIECES[LAST[0]]
    held = pl.pallas_call(
        functools.partial(kernel, ky_count, kz_count),
        out_shape=(shape(3, 2, part, N), scalar_shape, shape(2, piece, N), shape(N, N), shape(N, N)),
        in_specs=[pl.BlockSpec(memory_space=pltpu.SMEM), pl.BlockSpec(memory_space=pl.ANY)],
        out_specs=(vmem,) * 5,
        scratch_shapes=[
            in_vmem(4, 2, N, part),
            in_vmem(4, 2, ky_count // 2, rows, part),
            in_vmem(2, N, part),
            in_vmem(2, N // 2, part),
            in_vmem(3, kz_count, 2, part, part),
            in_vmem(3, 2, part, N),
            pltpu.VMEM((4, LOW, N), F32),
            pltpu.VMEM((4, LOW, N), F32),
            in_vmem(N, N),
            in_vmem(N, N),
            pltpu.SemaphoreType.REGULAR((ROUNDS,)),
            dma(4),
            dma(4),
            dma(4),
            dma(4),
            dma(4),
            dma(4),
            dma(3, most),
            dma(3, most),
            dma(3, most),
            pltpu.SemaphoreType.DMA,
            pltpu.SemaphoreType.DMA,
            pltpu.SemaphoreType.DMA,
            pltpu.SemaphoreType.DMA,
            dma(2),
        ],
        compiler_params=pltpu.CompilerParams(
            collective_id=0, has_side_effects=True, vmem_limit_bytes=44 * 2**20
        ),
        name="roll_and_transform",
    )(offsets, fields)
    return pl.pallas_call(
        functools.partial(finish, kz_count),
        out_shape=(shape(3, 2, 1, part, N), scalar_shape),
        in_specs=[vmem] * 5,
        out_specs=(hbm, hbm),
        scratch_shapes=[in_vmem(2, piece, N), dma(4)],
        compiler_params=pltpu.CompilerParams(vmem_limit_bytes=8 * 2**20),
        name="finish",
    )(*held)


def solution(mesh):
    placed = (P(None, None, None, "ky", "kz"), P())
    return jax.shard_map(
        shards,
        mesh=mesh,
        in_specs=placed,
        out_specs=(P(None, None, "ky", "kz", None), P(None, None, "ky", "kz")),
        check_vma=False,
    )
```

```python
import functools
import math

import jax
import jax.numpy as jnp
from jax import lax
from jax.experimental import pallas as pl
from jax.experimental.pallas import tpu as pltpu
from jax.sharding import PartitionSpec as P

N = 1024
LOW = 32
SCALE = 1.0 / math.sqrt(N)
MESH = pl.DeviceIdType.MESH
BF16 = jnp.bfloat16
F32 = jnp.float32
SCALAR = 3
PIECES = (1, 1, 4)
FIRST = (0, 1, 2)
LAST = (2, 3)
ROUNDS = 7


def dot(a, b):
    return jnp.dot(a, b, preferred_element_type=F32)


def along_z(half_ref, cos_ref, sin_ref, out_ref, blocks):
    size = half_ref.shape[1]
    width = N // blocks

    @pl.loop(0, blocks)
    def _(block):
        here = pl.ds(pl.multiple_of(block * width, width), width)
        both = half_ref[...].reshape(2 * size, N)
        by_cos, by_sin = dot(both, cos_ref[:, here]), dot(both, sin_ref[:, here])
        out_ref[0, :, here] = (by_cos[:size] - by_sin[size:]).astype(BF16)
        out_ref[1, :, here] = (by_sin[:size] + by_cos[size:]).astype(BF16)


def finish(blocks, velocity_ref, scalar_ref, last_ref, cos_ref, sin_ref, velocity_out, scalar_out, result, sems):
    size = last_ref.shape[1]
    done = pl.ds(0, N // blocks - size)
    copies = [
        pltpu.make_async_copy(velocity_ref.at[0:2], velocity_out.at[0:2, :, 0], sems.at[0]),
        pltpu.make_async_copy(velocity_ref.at[2, :, done], velocity_out.at[2, :, 0, done], sems.at[1]),
        pltpu.make_async_copy(scalar_ref, scalar_out, sems.at[2]),
        pltpu.make_async_copy(result, velocity_out.at[2, :, 0, pl.ds(N // blocks - size, size)], sems.at[3]),
    ]
    for copy in copies[:3]:
        copy.start()
    along_z(last_ref, cos_ref, sin_ref, result, blocks)
    copies[3].start()
    for copy in copies:
        copy.wait()


def kernel(
    ky_count,
    kz_count,
    offsets_hbm,
    fields_ref,
    velocity_ref,
    scalar_ref,
    last_ref,
    kz_cos,
    kz_sin,
    offsets_ref,
    gathered,
    relay,
    rolled,
    back_relay,
    half_done,
    across,
    factor,
    turned,
    ky_cos,
    ky_sin,
    word,
    offsets_sem,
    relay_send,
    relay_recv,
    relay_own,
    gather_send,
    gather_recv,
    own_sem,
    kz_send,
    kz_recv,
    kz_own,
    over_send,
    over_recv,
    back_send,
    back_recv,
    back_own,
):
    ky = lax.axis_index("ky")
    kz = lax.axis_index("kz")
    rows = N // ky_count
    part = N // kz_count
    plane_count = ky_count // 2

    x, low_z, y = lax.rem(ky, 4), lax.rem(ky // 4, 2), ky // 8

    def at(new_y, new_low_z, new_x):
        return lax.rem(new_y, 4) * 8 + new_low_z * 4 + lax.rem(new_x, 4)

    partner = at(y, 1 - low_z, x)

    def each_beside_x(act):
        pl.when(x > 0)(lambda: act(at(y, low_z, x + 3)))
        pl.when(x < 3)(lambda: act(at(y, low_z, x + 1)))

    def each_beside_y(act):
        pl.when(y > 0)(lambda: act(at(y + 3, low_z, x)))
        pl.when(y < 3)(lambda: act(at(y + 1, low_z, x)))

    def count_beside(place):
        return 2 - jnp.where(place == 0, 1, 0) - jnp.where(place == 3, 1, 0)

    def kz_peers():
        return [lax.rem(kz // 2 + step // 2, 2) * 2 + lax.rem(kz + step, 2) for step in (2, 3, 1)]

    def signal(sem, **device):
        pl.semaphore_signal(sem, inc=1, device_id=device, device_id_type=MESH)

    def remote(src, dst, send_sem, recv_sem, **device):
        return pltpu.make_async_remote_copy(
            src_ref=src, dst_ref=dst, send_sem=send_sem, recv_sem=recv_sem, device_id=device, device_id_type=MESH
        )

    barrier = pltpu.get_barrier_semaphore()
    signal(barrier, ky=partner)
    each_beside_x(lambda peer: signal(barrier, ky=peer))
    each_beside_y(lambda peer: signal(barrier, ky=peer))
    for peer in kz_peers():
        signal(barrier, kz=peer)
    pl.semaphore_wait(barrier, 4 + count_beside(x) + count_beside(y))

    def send_over(field):
        for group in range(4):
            remote(
                fields_ref.at[field, :, pl.ds(group * 8 + (1 - low_z) * 4, 4)],
                relay.at[field, :, pl.ds(group * 4, 4)],
                relay_send,
                relay_recv.at[field],
                ky=partner,
            ).start()

    def all_over(field):
        return remote(relay.at[field], relay.at[field], relay_send, relay_recv.at[field], ky=partner)

    for field in (SCALAR, 0, 1, 2):
        send_over(field)

    copy_offsets = pltpu.make_async_copy(offsets_hbm, offsets_ref, offsets_sem)
    copy_offsets.start()

    for index in range(3):
        each_beside_x(lambda peer: signal(word.at[index], ky=peer))
        pl.semaphore_wait(word.at[index], count_beside(x))
    for index in range(3, 6):
        each_beside_y(lambda peer: signal(word.at[index], ky=peer))
        pl.semaphore_wait(word.at[index], count_beside(y))
    signal(word.at[6], ky=partner)
    pl.semaphore_wait(word.at[6], 1)

    def rows_of(block):
        return pl.ds(pl.multiple_of(block * rows, rows), rows)

    my_rows, partner_rows = rows_of(ky), rows_of(partner)

    def in_plane(step):
        number = lax.rem(mine + step, plane_count)
        return number, at(number // 4, low_z, number)

    mine = y * 4 + x

    def own_copy(field):
        return pltpu.make_async_copy(fields_ref.at[field, :, ky], gathered.at[field, :, my_rows], own_sem.at[field])

    def relay_copy(field):
        return pltpu.make_async_copy(
            relay.at[field, :, mine], gathered.at[field, :, partner_rows], relay_own.at[field]
        )

    def gather(field):
        own_copy(field).start()

        @pl.loop(1, plane_count)
        def _(step):
            _, peer = in_plane(step)
            remote(
                fields_ref.at[field, :, peer],
                gathered.at[field, :, my_rows],
                gather_send,
                gather_recv.at[field],
                ky=peer,
            ).start()

    def pass_on(field):
        all_over(field).wait_recv()
        relay_copy(field).start()

        @pl.loop(1, plane_count)
        def _(step):
            number, peer = in_plane(step)
            remote(
                relay.at[field, :, number],
                gathered.at[field, :, partner_rows],
                gather_send,
                gather_recv.at[field],
                ky=peer,
            ).start()

    def gather_all(field):
        others = gathered.at[field, :, pl.ds(0, (ky_count - 2) * rows)]
        return remote(others, others, gather_send, gather_recv.at[field], ky=partner)

    def wait_gathered(field):
        own_copy(field).wait()
        relay_copy(field).wait()
        gather_all(field).wait_recv()

    gather(SCALAR)
    gather(0)

    copy_offsets.wait()
    offset = offsets_ref[ky]
    some = LOW // 4

    @pl.loop(0, 4)
    def _(group):
        here = pl.ds(pl.multiple_of(group * some, some), some)
        row = group * some + lax.broadcasted_iota(jnp.int32, (some, N), 0)
        column = lax.broadcasted_iota(jnp.int32, (some, N), 1)
        low_row = group * some + lax.broadcasted_iota(jnp.int32, (some, 128), 0)

        def wave(turns):
            angle = lax.rem(turns, N).astype(F32) * (2.0 * math.pi / N)
            return jnp.cos(angle), jnp.sin(angle)

        for index, multiple, scale in ((0, LOW, SCALE), (2, 1, 1.0)):
            a, b = wave(row * multiple * column)
            a, b = a * scale, b * scale
            c, s = wave(low_row * multiple * offset)
            c, s = c[:, :1], s[:, :1]
            factor[index, here] = a
            factor[index + 1, here] = b
            turned[index, here] = a * c - b * s
            turned[index + 1, here] = a * s + b * c

    def fill(source, cos_table, sin_table):
        @pl.loop(0, N // LOW)
        def _(block):
            a = source[0, pl.ds(block, 1)]
            b = source[1, pl.ds(block, 1)]
            c, s = source[2], source[3]
            here = pl.ds(pl.multiple_of(block * LOW, LOW), LOW)
            cos_table[here] = (a * c - b * s).astype(BF16)
            sin_table[here] = (a * s + b * c).astype(BF16)

    fill(turned, ky_cos, ky_sin)

    pass_on(SCALAR)
    gather(1)
    fill(factor, kz_cos, kz_sin)
    pass_on(0)
    gather(2)

    wait_gathered(SCALAR)

    @pl.loop(0, kz_count)
    def _(block):
        here = pl.ds(pl.multiple_of(block * part, part), part)
        target = block * part + lax.broadcasted_iota(jnp.int32, (part, N), 0)
        source = lax.rem(target + (N - offset), N)
        chosen = (lax.broadcasted_iota(jnp.int32, (part, N), 1) == source).astype(F32).astype(BF16)
        for side in range(2):
            rolled[side, here] = dot(chosen, gathered[SCALAR, side]).astype(BF16)

    for group in range(4):
        remote(
            rolled.at[:, pl.ds(pl.multiple_of(group * 256 + (1 - low_z) * 128, 128), 128)],
            back_relay.at[:, pl.ds(group * 128, 128)],
            over_send,
            over_recv,
            ky=partner,
        ).start()

    own_back = pltpu.make_async_copy(rolled.at[:, my_rows], scalar_ref.at[:, ky], back_own.at[0])
    own_back.start()

    @pl.loop(1, plane_count)
    def _(step):
        _, peer = in_plane(step)
        remote(rolled.at[:, rows_of(peer)], scalar_ref.at[:, ky], back_send, back_recv, ky=peer).start()

    my_part = pl.ds(pl.multiple_of(kz * part, part), part)

    def piece_rows(field, piece):
        size = part // PIECES[field]
        return pl.ds(piece * size, size)

    def own_across(field, piece):
        some_rows = piece_rows(field, piece)
        return pltpu.make_async_copy(
            half_done.at[field, kz, :, some_rows], across.at[field, :, some_rows, my_part], kz_own.at[FIRST[field] + piece]
        )

    def all_across(field, piece):
        others = across.at[field, :, piece_rows(field, piece), pl.ds(0, N - part)]
        return remote(others, others, kz_send, kz_recv.at[FIRST[field] + piece], kz=kz_peers()[0])

    for field in range(3):
        if field:
            pass_on(field)
        wait_gathered(field)

        @pl.loop(0, kz_count)
        def _(block):
            here = pl.ds(pl.multiple_of(block * part, part), part)
            c, s = ky_cos[here], ky_sin[here]
            real, imag = gathered[field, 0], gathered[field, 1]
            half_done[field, block, 0] = (dot(c, real) - dot(s, imag)).astype(BF16)
            half_done[field, block, 1] = (dot(s, real) + dot(c, imag)).astype(BF16)

        for piece in range(PIECES[field]):
            some_rows = piece_rows(field, piece)
            for peer in kz_peers():
                remote(
                    half_done.at[field, peer, :, some_rows],
                    across.at[field, :, some_rows, my_part],
                    kz_send,
                    kz_recv.at[FIRST[field] + piece],
                    kz=peer,
                ).start()
            own_across(field, piece).start()

    over = remote(back_relay, back_relay, over_send, over_recv, ky=partner)
    over.wait_recv()
    relay_back = pltpu.make_async_copy(back_relay.at[:, rows_of(mine)], scalar_ref.at[:, partner], back_own.at[1])
    relay_back.start()

    @pl.loop(1, plane_count)
    def _(step):
        number, peer = in_plane(step)
        remote(back_relay.at[:, rows_of(number)], scalar_ref.at[:, partner], back_send, back_recv, ky=peer).start()

    for field in range(3):
        for piece in range(PIECES[field]):
            own_across(field, piece).wait()
            all_across(field, piece).wait_recv()
            if (field, piece) != LAST:
                some_rows = piece_rows(field, piece)
                along_z(
                    across.at[field, :, some_rows], kz_cos, kz_sin, velocity_ref.at[field, :, some_rows], kz_count
                )

    last_ref[...] = across[LAST[0], :, piece_rows(*LAST)]
    others_back = scalar_ref.at[:, pl.ds(0, ky_count - 2)]
    back = remote(others_back, others_back, back_send, back_recv, ky=partner)
    back.wait_recv()
    own_back.wait()
    relay_back.wait()
    remote(relay, relay, relay_send, relay_recv.at[0], ky=partner).wait_send()
    sent = gathered.at[:, :, pl.ds(0, (ky_count - 2) * rows)]
    remote(sent, sent, gather_send, gather_recv.at[0], ky=partner).wait_send()
    sent = across.at[:, :, :, pl.ds(0, N - part)]
    remote(sent, sent, kz_send, kz_recv.at[0], kz=kz_peers()[0]).wait_send()
    over.wait_send()
    back.wait_send()


def shards(fields, offsets):
    ky_count, kz_count = lax.axis_size("ky"), lax.axis_size("kz")
    rows, part = fields.shape[3], fields.shape[4]
    in_vmem = lambda *shape: pltpu.VMEM(shape, BF16)
    dma = lambda *shape: pltpu.SemaphoreType.DMA(shape)
    vmem, hbm = pl.BlockSpec(memory_space=pltpu.VMEM), pl.BlockSpec(memory_space=pltpu.HBM)
    shape = lambda *dims: jax.ShapeDtypeStruct(dims, BF16)
    scalar_shape = shape(2, ky_count, rows, part)
    piece = part // PIECES[LAST[0]]
    held = pl.pallas_call(
        functools.partial(kernel, ky_count, kz_count),
        out_shape=(shape(3, 2, part, N), scalar_shape, shape(2, piece, N), shape(N, N), shape(N, N)),
        in_specs=[hbm, pl.BlockSpec(memory_space=pl.ANY)],
        out_specs=(vmem,) * 5,
        scratch_shapes=[
            pltpu.SMEM((ky_count,), jnp.int32),
            in_vmem(4, 2, N, part),
            in_vmem(4, 2, ky_count // 2, rows, part),
            in_vmem(2, N, part),
            in_vmem(2, N // 2, part),
            in_vmem(3, kz_count, 2, part, part),
            in_vmem(3, 2, part, N),
            pltpu.VMEM((4, LOW, N), F32),
            pltpu.VMEM((4, LOW, N), F32),
            in_vmem(N, N),
            in_vmem(N, N),
            pltpu.SemaphoreType.REGULAR((ROUNDS,)),
            pltpu.SemaphoreType.DMA,
            pltpu.SemaphoreType.DMA,
            dma(4),
            dma(4),
            pltpu.SemaphoreType.DMA,
            dma(4),
            dma(4),
            pltpu.SemaphoreType.DMA,
            dma(sum(PIECES)),
            dma(sum(PIECES)),
            pltpu.SemaphoreType.DMA,
            pltpu.SemaphoreType.DMA,
            pltpu.SemaphoreType.DMA,
            pltpu.SemaphoreType.DMA,
            dma(2),
        ],
        compiler_params=pltpu.CompilerParams(
            collective_id=0, has_side_effects=True, vmem_limit_bytes=44 * 2**20
        ),
        name="roll_and_transform",
    )(offsets, fields)
    return pl.pallas_call(
        functools.partial(finish, kz_count),
        out_shape=(shape(3, 2, 1, part, N), scalar_shape),
        in_specs=[vmem] * 5,
        out_specs=(hbm, hbm),
        scratch_shapes=[in_vmem(2, piece, N), dma(4)],
        compiler_params=pltpu.CompilerParams(vmem_limit_bytes=8 * 2**20),
        name="finish",
    )(*held)


def solution(mesh):
    placed = (P(None, None, None, "ky", "kz"), P())
    return jax.shard_map(
        shards,
        mesh=mesh,
        in_specs=placed,
        out_specs=(P(None, None, "ky", "kz", None), P(None, None, "ky", "kz")),
        check_vma=False,
    )
```

```python
import functools
import math

import jax
import jax.numpy as jnp
from jax import lax
from jax.experimental import pallas as pl
from jax.experimental.pallas import tpu as pltpu
from jax.sharding import PartitionSpec as P

N = 1024
LOW = 32
SCALE = 1.0 / math.sqrt(N)
MESH = pl.DeviceIdType.MESH
BF16 = jnp.bfloat16
F32 = jnp.float32
SCALAR = 3
PIECES = (1, 1, 4)
FIRST = (0, 1, 2)
LAST = (2, 3)
ROUNDS = 7


def dot(a, b):
    return jnp.dot(a, b, preferred_element_type=F32)


def along_z(half_ref, cos_ref, sin_ref, out_ref, blocks):
    size = half_ref.shape[1]
    width = N // blocks

    @pl.loop(0, blocks)
    def _(block):
        here = pl.ds(pl.multiple_of(block * width, width), width)
        both = half_ref[...].reshape(2 * size, N)
        by_cos, by_sin = dot(both, cos_ref[:, here]), dot(both, sin_ref[:, here])
        out_ref[0, :, here] = (by_cos[:size] - by_sin[size:]).astype(BF16)
        out_ref[1, :, here] = (by_sin[:size] + by_cos[size:]).astype(BF16)


def finish(blocks, velocity_ref, scalar_ref, last_ref, cos_ref, sin_ref, velocity_out, scalar_out, result, sems):
    size = last_ref.shape[1]
    done = pl.ds(0, N // blocks - size)
    copies = [
        pltpu.make_async_copy(velocity_ref.at[0:2], velocity_out.at[0:2, :, 0], sems.at[0]),
        pltpu.make_async_copy(velocity_ref.at[2, :, done], velocity_out.at[2, :, 0, done], sems.at[1]),
        pltpu.make_async_copy(scalar_ref, scalar_out, sems.at[2]),
        pltpu.make_async_copy(result, velocity_out.at[2, :, 0, pl.ds(N // blocks - size, size)], sems.at[3]),
    ]
    for copy in copies[:3]:
        copy.start()
    along_z(last_ref, cos_ref, sin_ref, result, blocks)
    copies[3].start()
    for copy in copies:
        copy.wait()


def kernel(
    ky_count,
    kz_count,
    offsets_hbm,
    fields_ref,
    velocity_ref,
    scalar_ref,
    last_ref,
    kz_cos,
    kz_sin,
    offsets_ref,
    gathered,
    relay,
    rolled,
    back_relay,
    half_done,
    across,
    factor,
    turned,
    ky_cos,
    ky_sin,
    word,
    offsets_sem,
    relay_send,
    relay_recv,
    relay_own,
    gather_send,
    gather_recv,
    own_sem,
    kz_send,
    kz_recv,
    kz_own,
    over_send,
    over_recv,
    back_send,
    back_recv,
    back_own,
):
    ky = lax.axis_index("ky")
    kz = lax.axis_index("kz")
    rows = N // ky_count
    part = N // kz_count
    plane_count = ky_count // 2

    x, low_z, y = lax.rem(ky, 4), lax.rem(ky // 4, 2), ky // 8

    def at(new_y, new_low_z, new_x):
        return lax.rem(new_y, 4) * 8 + new_low_z * 4 + lax.rem(new_x, 4)

    partner = at(y, 1 - low_z, x)

    def each_beside_x(act):
        pl.when(x > 0)(lambda: act(at(y, low_z, x + 3)))
        pl.when(x < 3)(lambda: act(at(y, low_z, x + 1)))

    def each_beside_y(act):
        pl.when(y > 0)(lambda: act(at(y + 3, low_z, x)))
        pl.when(y < 3)(lambda: act(at(y + 1, low_z, x)))

    def count_beside(place):
        return 2 - jnp.where(place == 0, 1, 0) - jnp.where(place == 3, 1, 0)

    def kz_peers():
        return [lax.rem(kz // 2 + step // 2, 2) * 2 + lax.rem(kz + step, 2) for step in (2, 3, 1)]

    def signal(sem, **device):
        pl.semaphore_signal(sem, inc=1, device_id=device, device_id_type=MESH)

    def remote(src, dst, send_sem, recv_sem, **device):
        return pltpu.make_async_remote_copy(
            src_ref=src, dst_ref=dst, send_sem=send_sem, recv_sem=recv_sem, device_id=device, device_id_type=MESH
        )

    barrier = pltpu.get_barrier_semaphore()
    signal(barrier, ky=partner)
    each_beside_x(lambda peer: signal(barrier, ky=peer))
    each_beside_y(lambda peer: signal(barrier, ky=peer))
    for peer in kz_peers():
        signal(barrier, kz=peer)
    pl.semaphore_wait(barrier, 4 + count_beside(x) + count_beside(y))

    def send_over(field):
        for group in range(4):
            remote(
                fields_ref.at[field, :, pl.ds(group * 8 + (1 - low_z) * 4, 4)],
                relay.at[field, :, pl.ds(group * 4, 4)],
                relay_send,
                relay_recv.at[field],
                ky=partner,
            ).start()

    def all_over(field):
        return remote(relay.at[field], relay.at[field], relay_send, relay_recv.at[field], ky=partner)

    for field in (SCALAR, 0, 1, 2):
        send_over(field)

    copy_offsets = pltpu.make_async_copy(offsets_hbm, offsets_ref, offsets_sem)
    copy_offsets.start()

    for index in range(3):
        each_beside_x(lambda peer: signal(word.at[index], ky=peer))
        pl.semaphore_wait(word.at[index], count_beside(x))
    for index in range(3, 6):
        each_beside_y(lambda peer: signal(word.at[index], ky=peer))
        pl.semaphore_wait(word.at[index], count_beside(y))
    signal(word.at[6], ky=partner)
    pl.semaphore_wait(word.at[6], 1)

    def rows_of(block):
        return pl.ds(pl.multiple_of(block * rows, rows), rows)

    my_rows, partner_rows = rows_of(ky), rows_of(partner)

    def in_plane(step):
        number = lax.rem(mine + step, plane_count)
        return number, at(number // 4, low_z, number)

    mine = y * 4 + x

    def own_copy(field):
        return pltpu.make_async_copy(fields_ref.at[field, :, ky], gathered.at[field, :, my_rows], own_sem.at[field])

    def relay_copy(field):
        return pltpu.make_async_copy(
            relay.at[field, :, mine], gathered.at[field, :, partner_rows], relay_own.at[field]
        )

    def gather(field):
        own_copy(field).start()

        @pl.loop(1, plane_count)
        def _(step):
            _, peer = in_plane(step)
            remote(
                fields_ref.at[field, :, peer],
                gathered.at[field, :, my_rows],
                gather_send,
                gather_recv.at[field],
                ky=peer,
            ).start()

    def pass_on(field):
        all_over(field).wait_recv()
        relay_copy(field).start()

        @pl.loop(1, plane_count)
        def _(step):
            number, peer = in_plane(step)
            remote(
                relay.at[field, :, number],
                gathered.at[field, :, partner_rows],
                gather_send,
                gather_recv.at[field],
                ky=peer,
            ).start()

    def gather_all(field):
        others = gathered.at[field, :, pl.ds(0, (ky_count - 2) * rows)]
        return remote(others, others, gather_send, gather_recv.at[field], ky=partner)

    def wait_gathered(field):
        own_copy(field).wait()
        relay_copy(field).wait()
        gather_all(field).wait_recv()

    gather(SCALAR)
    gather(0)

    copy_offsets.wait()
    offset = offsets_ref[ky]
    some = LOW // 4

    @pl.loop(0, 4)
    def _(group):
        here = pl.ds(pl.multiple_of(group * some, some), some)
        row = group * some + lax.broadcasted_iota(jnp.int32, (some, N), 0)
        column = lax.broadcasted_iota(jnp.int32, (some, N), 1)
        low_row = group * some + lax.broadcasted_iota(jnp.int32, (some, 128), 0)

        def wave(turns):
            angle = lax.rem(turns, N).astype(F32) * (2.0 * math.pi / N)
            return jnp.cos(angle), jnp.sin(angle)

        for index, multiple, scale in ((0, LOW, SCALE), (2, 1, 1.0)):
            a, b = wave(row * multiple * column)
            a, b = a * scale, b * scale
            c, s = wave(low_row * multiple * offset)
            c, s = c[:, :1], s[:, :1]
            factor[index, here] = a
            factor[index + 1, here] = b
            turned[index, here] = a * c - b * s
            turned[index + 1, here] = a * s + b * c

    def fill(source, cos_table, sin_table):
        @pl.loop(0, N // LOW)
        def _(block):
            a = source[0, pl.ds(block, 1)]
            b = source[1, pl.ds(block, 1)]
            c, s = source[2], source[3]
            here = pl.ds(pl.multiple_of(block * LOW, LOW), LOW)
            cos_table[here] = (a * c - b * s).astype(BF16)
            sin_table[here] = (a * s + b * c).astype(BF16)

    fill(turned, ky_cos, ky_sin)

    pass_on(SCALAR)
    gather(1)
    fill(factor, kz_cos, kz_sin)
    pass_on(0)
    gather(2)

    wait_gathered(SCALAR)

    @pl.loop(0, kz_count)
    def _(block):
        here = pl.ds(pl.multiple_of(block * part, part), part)
        target = block * part + lax.broadcasted_iota(jnp.int32, (part, N), 0)
        source = lax.rem(target + (N - offset), N)
        chosen = (lax.broadcasted_iota(jnp.int32, (part, N), 1) == source).astype(F32).astype(BF16)
        for side in range(2):
            rolled[side, here] = dot(chosen, gathered[SCALAR, side]).astype(BF16)

    for group in range(4):
        remote(
            rolled.at[:, pl.ds(pl.multiple_of(group * 256 + (1 - low_z) * 128, 128), 128)],
            back_relay.at[:, pl.ds(group * 128, 128)],
            over_send,
            over_recv,
            ky=partner,
        ).start()

    own_back = pltpu.make_async_copy(rolled.at[:, my_rows], scalar_ref.at[:, ky], back_own.at[0])
    own_back.start()

    @pl.loop(1, plane_count)
    def _(step):
        _, peer = in_plane(step)
        remote(rolled.at[:, rows_of(peer)], scalar_ref.at[:, ky], back_send, back_recv, ky=peer).start()

    my_part = pl.ds(pl.multiple_of(kz * part, part), part)

    def piece_rows(field, piece):
        size = part // PIECES[field]
        return pl.ds(piece * size, size)

    def own_across(field, piece):
        some_rows = piece_rows(field, piece)
        return pltpu.make_async_copy(
            half_done.at[field, kz, :, some_rows], across.at[field, :, some_rows, my_part], kz_own.at[FIRST[field] + piece]
        )

    def all_across(field, piece):
        others = across.at[field, :, piece_rows(field, piece), pl.ds(0, N - part)]
        return remote(others, others, kz_send, kz_recv.at[FIRST[field] + piece], kz=kz_peers()[0])

    for field in range(3):
        if field:
            pass_on(field)
        wait_gathered(field)

        @pl.loop(0, kz_count)
        def _(block):
            here = pl.ds(pl.multiple_of(block * part, part), part)
            c, s = ky_cos[here], ky_sin[here]
            real, imag = gathered[field, 0], gathered[field, 1]
            half_done[field, block, 0] = (dot(c, real) - dot(s, imag)).astype(BF16)
            half_done[field, block, 1] = (dot(s, real) + dot(c, imag)).astype(BF16)

        for piece in range(PIECES[field]):
            some_rows = piece_rows(field, piece)
            for peer in kz_peers():
                remote(
                    half_done.at[field, peer, :, some_rows],
                    across.at[field, :, some_rows, my_part],
                    kz_send,
                    kz_recv.at[FIRST[field] + piece],
                    kz=peer,
                ).start()
            own_across(field, piece).start()

    over = remote(back_relay, back_relay, over_send, over_recv, ky=partner)
    over.wait_recv()
    relay_back = pltpu.make_async_copy(back_relay.at[:, rows_of(mine)], scalar_ref.at[:, partner], back_own.at[1])
    relay_back.start()

    @pl.loop(1, plane_count)
    def _(step):
        number, peer = in_plane(step)
        remote(back_relay.at[:, rows_of(number)], scalar_ref.at[:, partner], back_send, back_recv, ky=peer).start()

    for field in range(3):
        for piece in range(PIECES[field]):
            own_across(field, piece).wait()
            all_across(field, piece).wait_recv()
            if (field, piece) != LAST:
                some_rows = piece_rows(field, piece)
                along_z(
                    across.at[field, :, some_rows], kz_cos, kz_sin, velocity_ref.at[field, :, some_rows], kz_count
                )

    last_ref[...] = across[LAST[0], :, piece_rows(*LAST)]
    others_back = scalar_ref.at[:, pl.ds(0, ky_count - 2)]
    back = remote(others_back, others_back, back_send, back_recv, ky=partner)
    back.wait_recv()
    own_back.wait()
    relay_back.wait()
    remote(relay, relay, relay_send, relay_recv.at[0], ky=partner).wait_send()
    sent = gathered.at[:, :, pl.ds(0, (ky_count - 2) * rows)]
    remote(sent, sent, gather_send, gather_recv.at[0], ky=partner).wait_send()
    sent = across.at[:, :, :, pl.ds(0, N - part)]
    remote(sent, sent, kz_send, kz_recv.at[0], kz=kz_peers()[0]).wait_send()
    over.wait_send()
    back.wait_send()


def shards(fields, offsets):
    ky_count, kz_count = lax.axis_size("ky"), lax.axis_size("kz")
    rows, part = fields.shape[3], fields.shape[4]
    in_hbm = lambda array: pltpu.with_memory_space_constraint(array, pltpu.HBM)
    in_vmem = lambda *shape: pltpu.VMEM(shape, BF16)
    dma = lambda *shape: pltpu.SemaphoreType.DMA(shape)
    vmem, hbm = pl.BlockSpec(memory_space=pltpu.VMEM), pl.BlockSpec(memory_space=pltpu.HBM)
    shape = lambda *dims: jax.ShapeDtypeStruct(dims, BF16)
    scalar_shape = shape(2, ky_count, rows, part)
    piece = part // PIECES[LAST[0]]
    held = pl.pallas_call(
        functools.partial(kernel, ky_count, kz_count),
        out_shape=(shape(3, 2, part, N), scalar_shape, shape(2, piece, N), shape(N, N), shape(N, N)),
        in_specs=[hbm, pl.BlockSpec(memory_space=pl.ANY)],
        out_specs=(vmem,) * 5,
        scratch_shapes=[
            pltpu.SMEM((ky_count,), jnp.int32),
            in_vmem(4, 2, N, part),
            in_vmem(4, 2, ky_count // 2, rows, part),
            in_vmem(2, N, part),
            in_vmem(2, N // 2, part),
            in_vmem(3, kz_count, 2, part, part),
            in_vmem(3, 2, part, N),
            pltpu.VMEM((4, LOW, N), F32),
            pltpu.VMEM((4, LOW, N), F32),
            in_vmem(N, N),
            in_vmem(N, N),
            pltpu.SemaphoreType.REGULAR((ROUNDS,)),
            pltpu.SemaphoreType.DMA,
            pltpu.SemaphoreType.DMA,
            dma(4),
            dma(4),
            pltpu.SemaphoreType.DMA,
            dma(4),
            dma(4),
            pltpu.SemaphoreType.DMA,
            dma(sum(PIECES)),
            dma(sum(PIECES)),
            pltpu.SemaphoreType.DMA,
            pltpu.SemaphoreType.DMA,
            pltpu.SemaphoreType.DMA,
            pltpu.SemaphoreType.DMA,
            dma(2),
        ],
        compiler_params=pltpu.CompilerParams(
            collective_id=0, has_side_effects=True, vmem_limit_bytes=44 * 2**20
        ),
        name="roll_and_transform",
    )(in_hbm(offsets), in_hbm(fields))
    return pl.pallas_call(
        functools.partial(finish, kz_count),
        out_shape=(shape(3, 2, 1, part, N), scalar_shape),
        in_specs=[vmem] * 5,
        out_specs=(hbm, hbm),
        scratch_shapes=[in_vmem(2, piece, N), dma(4)],
        compiler_params=pltpu.CompilerParams(vmem_limit_bytes=8 * 2**20),
        name="finish",
    )(*held)


def solution(mesh):
    placed = (P(None, None, None, "ky", "kz"), P())
    return jax.shard_map(
        shards,
        mesh=mesh,
        in_specs=placed,
        out_specs=(P(None, None, "ky", "kz", None), P(None, None, "ky", "kz")),
        check_vma=False,
    )
```

```python
import functools
import math

import jax
import jax.numpy as jnp
from jax import lax
from jax.experimental import pallas as pl
from jax.experimental.pallas import tpu as pltpu
from jax.sharding import PartitionSpec as P

N = 1024
LOW = 32
SCALE = 1.0 / math.sqrt(N)
MESH = pl.DeviceIdType.MESH
BF16 = jnp.bfloat16
F32 = jnp.float32
SCALAR = 3
PIECES = (1, 1, 4)
FIRST = (0, 1, 2)
LAST = (2, 3)
ROUNDS = 7


def dot(a, b):
    return jnp.dot(a, b, preferred_element_type=F32)


def along_z(half_ref, cos_ref, sin_ref, out_ref, blocks):
    size = half_ref.shape[1]
    width = N // blocks

    @pl.loop(0, blocks)
    def _(block):
        here = pl.ds(pl.multiple_of(block * width, width), width)
        both = half_ref[...].reshape(2 * size, N)
        by_cos, by_sin = dot(both, cos_ref[:, here]), dot(both, sin_ref[:, here])
        out_ref[0, :, here] = (by_cos[:size] - by_sin[size:]).astype(BF16)
        out_ref[1, :, here] = (by_sin[:size] + by_cos[size:]).astype(BF16)


def finish(blocks, velocity_ref, scalar_ref, last_ref, cos_ref, sin_ref, velocity_out, scalar_out, result, sems):
    size = last_ref.shape[1]
    done = pl.ds(0, N // blocks - size)
    copies = [
        pltpu.make_async_copy(velocity_ref.at[0:2], velocity_out.at[0:2, :, 0], sems.at[0]),
        pltpu.make_async_copy(velocity_ref.at[2, :, done], velocity_out.at[2, :, 0, done], sems.at[1]),
        pltpu.make_async_copy(scalar_ref, scalar_out, sems.at[2]),
        pltpu.make_async_copy(result, velocity_out.at[2, :, 0, pl.ds(N // blocks - size, size)], sems.at[3]),
    ]
    for copy in copies[:3]:
        copy.start()
    along_z(last_ref, cos_ref, sin_ref, result, blocks)
    copies[3].start()
    for copy in copies:
        copy.wait()


def kernel(
    ky_count,
    kz_count,
    offsets_hbm,
    fields_ref,
    velocity_ref,
    scalar_ref,
    last_ref,
    kz_cos,
    kz_sin,
    offsets_ref,
    gathered,
    relay,
    rolled,
    back_relay,
    half_done,
    across,
    factor,
    turned,
    ky_cos,
    ky_sin,
    word,
    offsets_sem,
    relay_send,
    relay_recv,
    relay_own,
    gather_send,
    gather_recv,
    own_sem,
    kz_send,
    kz_recv,
    kz_own,
    over_send,
    over_recv,
    back_send,
    back_recv,
    back_own,
):
    ky = lax.axis_index("ky")
    kz = lax.axis_index("kz")
    rows = N // ky_count
    part = N // kz_count
    plane_count = ky_count // 2

    x, low_z, y = lax.rem(ky, 4), lax.rem(ky // 4, 2), ky // 8

    def at(new_y, new_low_z, new_x):
        return lax.rem(new_y, 4) * 8 + new_low_z * 4 + lax.rem(new_x, 4)

    partner = at(y, 1 - low_z, x)

    def each_beside_x(act):
        pl.when(x > 0)(lambda: act(at(y, low_z, x + 3)))
        pl.when(x < 3)(lambda: act(at(y, low_z, x + 1)))

    def each_beside_y(act):
        pl.when(y > 0)(lambda: act(at(y + 3, low_z, x)))
        pl.when(y < 3)(lambda: act(at(y + 1, low_z, x)))

    def count_beside(place):
        return 2 - jnp.where(place == 0, 1, 0) - jnp.where(place == 3, 1, 0)

    def kz_peers():
        return [lax.rem(kz // 2 + step // 2, 2) * 2 + lax.rem(kz + step, 2) for step in (2, 3, 1)]

    def signal(sem, **device):
        pl.semaphore_signal(sem, inc=1, device_id=device, device_id_type=MESH)

    def remote(src, dst, send_sem, recv_sem, **device):
        return pltpu.make_async_remote_copy(
            src_ref=src, dst_ref=dst, send_sem=send_sem, recv_sem=recv_sem, device_id=device, device_id_type=MESH
        )

    barrier = pltpu.get_barrier_semaphore()
    signal(barrier, ky=partner)
    each_beside_x(lambda peer: signal(barrier, ky=peer))
    each_beside_y(lambda peer: signal(barrier, ky=peer))
    for peer in kz_peers():
        signal(barrier, kz=peer)
    pl.semaphore_wait(barrier, 4 + count_beside(x) + count_beside(y))

    def send_over(field):
        for group in range(4):
            remote(
                fields_ref.at[field, :, pl.ds(group * 8 + (1 - low_z) * 4, 4)],
                relay.at[field, :, pl.ds(group * 4, 4)],
                relay_send,
                relay_recv.at[field],
                ky=partner,
            ).start()

    def all_over(field):
        return remote(relay.at[field], relay.at[field], relay_send, relay_recv.at[field], ky=partner)

    for field in (SCALAR, 0, 1, 2):
        send_over(field)

    copy_offsets = pltpu.make_async_copy(offsets_hbm, offsets_ref, offsets_sem)
    copy_offsets.start()

    for index in range(3):
        each_beside_x(lambda peer: signal(word.at[index], ky=peer))
        pl.semaphore_wait(word.at[index], count_beside(x))
    for index in range(3, 6):
        each_beside_y(lambda peer: signal(word.at[index], ky=peer))
        pl.semaphore_wait(word.at[index], count_beside(y))
    signal(word.at[6], ky=partner)
    pl.semaphore_wait(word.at[6], 1)

    def rows_of(block):
        return pl.ds(pl.multiple_of(block * rows, rows), rows)

    my_rows, partner_rows = rows_of(ky), rows_of(partner)

    def in_plane(step):
        number = lax.rem(mine + step, plane_count)
        return number, at(number // 4, low_z, number)

    mine = y * 4 + x

    def own_copy(field):
        return pltpu.make_async_copy(fields_ref.at[field, :, ky], gathered.at[field, :, my_rows], own_sem.at[field])

    def relay_copy(field):
        return pltpu.make_async_copy(
            relay.at[field, :, mine], gathered.at[field, :, partner_rows], relay_own.at[field]
        )

    def gather(field):
        own_copy(field).start()

        @pl.loop(1, plane_count)
        def _(step):
            _, peer = in_plane(step)
            remote(
                fields_ref.at[field, :, peer],
                gathered.at[field, :, my_rows],
                gather_send,
                gather_recv.at[field],
                ky=peer,
            ).start()

    def pass_on(field):
        all_over(field).wait_recv()
        relay_copy(field).start()

        @pl.loop(1, plane_count)
        def _(step):
            number, peer = in_plane(step)
            remote(
                relay.at[field, :, number],
                gathered.at[field, :, partner_rows],
                gather_send,
                gather_recv.at[field],
                ky=peer,
            ).start()

    def gather_all(field):
        others = gathered.at[field, :, pl.ds(0, (ky_count - 2) * rows)]
        return remote(others, others, gather_send, gather_recv.at[field], ky=partner)

    def wait_gathered(field):
        own_copy(field).wait()
        relay_copy(field).wait()
        gather_all(field).wait_recv()

    gather(SCALAR)
    gather(0)

    copy_offsets.wait()
    offset = offsets_ref[ky]
    some = LOW // 4

    @pl.loop(0, 4)
    def _(group):
        here = pl.ds(pl.multiple_of(group * some, some), some)
        row = group * some + lax.broadcasted_iota(jnp.int32, (some, N), 0)
        column = lax.broadcasted_iota(jnp.int32, (some, N), 1)
        low_row = group * some + lax.broadcasted_iota(jnp.int32, (some, 128), 0)

        def wave(turns):
            angle = lax.rem(turns, N).astype(F32) * (2.0 * math.pi / N)
            return jnp.cos(angle), jnp.sin(angle)

        for index, multiple, scale in ((0, LOW, SCALE), (2, 1, 1.0)):
            a, b = wave(row * multiple * column)
            a, b = a * scale, b * scale
            c, s = wave(low_row * multiple * offset)
            c, s = c[:, :1], s[:, :1]
            factor[index, here] = a
            factor[index + 1, here] = b
            turned[index, here] = a * c - b * s
            turned[index + 1, here] = a * s + b * c

    def fill(source, cos_table, sin_table):
        @pl.loop(0, N // LOW)
        def _(block):
            a = source[0, pl.ds(block, 1)]
            b = source[1, pl.ds(block, 1)]
            c, s = source[2], source[3]
            here = pl.ds(pl.multiple_of(block * LOW, LOW), LOW)
            cos_table[here] = (a * c - b * s).astype(BF16)
            sin_table[here] = (a * s + b * c).astype(BF16)

    fill(turned, ky_cos, ky_sin)

    pass_on(SCALAR)
    gather(1)
    fill(factor, kz_cos, kz_sin)
    pass_on(0)
    gather(2)

    wait_gathered(SCALAR)

    @pl.loop(0, kz_count)
    def _(block):
        here = pl.ds(pl.multiple_of(block * part, part), part)
        target = block * part + lax.broadcasted_iota(jnp.int32, (part, N), 0)
        source = lax.rem(target + (N - offset), N)
        chosen = (lax.broadcasted_iota(jnp.int32, (part, N), 1) == source).astype(F32).astype(BF16)
        for side in range(2):
            rolled[side, here] = dot(chosen, gathered[SCALAR, side]).astype(BF16)

    for group in range(4):
        remote(
            rolled.at[:, pl.ds(pl.multiple_of(group * 256 + (1 - low_z) * 128, 128), 128)],
            back_relay.at[:, pl.ds(group * 128, 128)],
            over_send,
            over_recv,
            ky=partner,
        ).start()

    own_back = pltpu.make_async_copy(rolled.at[:, my_rows], scalar_ref.at[:, ky], back_own.at[0])
    own_back.start()

    @pl.loop(1, plane_count)
    def _(step):
        _, peer = in_plane(step)
        remote(rolled.at[:, rows_of(peer)], scalar_ref.at[:, ky], back_send, back_recv, ky=peer).start()

    my_part = pl.ds(pl.multiple_of(kz * part, part), part)

    def piece_rows(field, piece):
        size = part // PIECES[field]
        return pl.ds(piece * size, size)

    def own_across(field, piece):
        some_rows = piece_rows(field, piece)
        return pltpu.make_async_copy(
            half_done.at[field, kz, :, some_rows], across.at[field, :, some_rows, my_part], kz_own.at[FIRST[field] + piece]
        )

    def all_across(field, piece):
        others = across.at[field, :, piece_rows(field, piece), pl.ds(0, N - part)]
        return remote(others, others, kz_send, kz_recv.at[FIRST[field] + piece], kz=kz_peers()[0])

    for field in range(3):
        if field:
            pass_on(field)
        wait_gathered(field)

        @pl.loop(0, kz_count)
        def _(block):
            here = pl.ds(pl.multiple_of(block * part, part), part)
            c, s = ky_cos[here], ky_sin[here]
            real, imag = gathered[field, 0], gathered[field, 1]
            half_done[field, block, 0] = (dot(c, real) - dot(s, imag)).astype(BF16)
            half_done[field, block, 1] = (dot(s, real) + dot(c, imag)).astype(BF16)

        for piece in range(PIECES[field]):
            some_rows = piece_rows(field, piece)
            for peer in kz_peers():
                remote(
                    half_done.at[field, peer, :, some_rows],
                    across.at[field, :, some_rows, my_part],
                    kz_send,
                    kz_recv.at[FIRST[field] + piece],
                    kz=peer,
                ).start()
            own_across(field, piece).start()

    over = remote(back_relay, back_relay, over_send, over_recv, ky=partner)
    over.wait_recv()
    relay_back = pltpu.make_async_copy(back_relay.at[:, rows_of(mine)], scalar_ref.at[:, partner], back_own.at[1])
    relay_back.start()

    @pl.loop(1, plane_count)
    def _(step):
        number, peer = in_plane(step)
        remote(back_relay.at[:, rows_of(number)], scalar_ref.at[:, partner], back_send, back_recv, ky=peer).start()

    for field in range(3):
        for piece in range(PIECES[field]):
            if (field, piece) == LAST:
                others_back = scalar_ref.at[:, pl.ds(0, ky_count - 2)]
                back = remote(others_back, others_back, back_send, back_recv, ky=partner)
                back.wait_recv()
                own_back.wait()
                relay_back.wait()
                remote(relay, relay, relay_send, relay_recv.at[0], ky=partner).wait_send()
                sent = gathered.at[:, :, pl.ds(0, (ky_count - 2) * rows)]
                remote(sent, sent, gather_send, gather_recv.at[0], ky=partner).wait_send()
                over.wait_send()
                back.wait_send()

            own_across(field, piece).wait()
            all_across(field, piece).wait_recv()
            if (field, piece) != LAST:
                some_rows = piece_rows(field, piece)
                along_z(
                    across.at[field, :, some_rows], kz_cos, kz_sin, velocity_ref.at[field, :, some_rows], kz_count
                )

    last_ref[...] = across[LAST[0], :, piece_rows(*LAST)]
    sent = across.at[:, :, :, pl.ds(0, N - part)]
    remote(sent, sent, kz_send, kz_recv.at[0], kz=kz_peers()[0]).wait_send()


def shards(fields, offsets):
    ky_count, kz_count = lax.axis_size("ky"), lax.axis_size("kz")
    rows, part = fields.shape[3], fields.shape[4]
    in_hbm = lambda array: pltpu.with_memory_space_constraint(array, pltpu.HBM)
    in_vmem = lambda *shape: pltpu.VMEM(shape, BF16)
    dma = lambda *shape: pltpu.SemaphoreType.DMA(shape)
    vmem, hbm = pl.BlockSpec(memory_space=pltpu.VMEM), pl.BlockSpec(memory_space=pltpu.HBM)
    shape = lambda *dims: jax.ShapeDtypeStruct(dims, BF16)
    scalar_shape = shape(2, ky_count, rows, part)
    piece = part // PIECES[LAST[0]]
    held = pl.pallas_call(
        functools.partial(kernel, ky_count, kz_count),
        out_shape=(shape(3, 2, part, N), scalar_shape, shape(2, piece, N), shape(N, N), shape(N, N)),
        in_specs=[hbm, pl.BlockSpec(memory_space=pl.ANY)],
        out_specs=(vmem,) * 5,
        scratch_shapes=[
            pltpu.SMEM((ky_count,), jnp.int32),
            in_vmem(4, 2, N, part),
            in_vmem(4, 2, ky_count // 2, rows, part),
            in_vmem(2, N, part),
            in_vmem(2, N // 2, part),
            in_vmem(3, kz_count, 2, part, part),
            in_vmem(3, 2, part, N),
            pltpu.VMEM((4, LOW, N), F32),
            pltpu.VMEM((4, LOW, N), F32),
            in_vmem(N, N),
            in_vmem(N, N),
            pltpu.SemaphoreType.REGULAR((ROUNDS,)),
            pltpu.SemaphoreType.DMA,
            pltpu.SemaphoreType.DMA,
            dma(4),
            dma(4),
            pltpu.SemaphoreType.DMA,
            dma(4),
            dma(4),
            pltpu.SemaphoreType.DMA,
            dma(sum(PIECES)),
            dma(sum(PIECES)),
            pltpu.SemaphoreType.DMA,
            pltpu.SemaphoreType.DMA,
            pltpu.SemaphoreType.DMA,
            pltpu.SemaphoreType.DMA,
            dma(2),
        ],
        compiler_params=pltpu.CompilerParams(
            collective_id=0, has_side_effects=True, vmem_limit_bytes=44 * 2**20
        ),
        name="roll_and_transform",
    )(in_hbm(offsets), in_hbm(fields))
    return pl.pallas_call(
        functools.partial(finish, kz_count),
        out_shape=(shape(3, 2, 1, part, N), scalar_shape),
        in_specs=[vmem] * 5,
        out_specs=(hbm, hbm),
        scratch_shapes=[in_vmem(2, piece, N), dma(4)],
        compiler_params=pltpu.CompilerParams(vmem_limit_bytes=8 * 2**20),
        name="finish",
    )(*held)


def solution(mesh):
    placed = (P(None, None, None, "ky", "kz"), P())
    return jax.shard_map(
        shards,
        mesh=mesh,
        in_specs=placed,
        out_specs=(P(None, None, "ky", "kz", None), P(None, None, "ky", "kz")),
        check_vma=False,
    )
```

```python
import functools
import math

import jax
import jax.numpy as jnp
from jax import lax
from jax.experimental import pallas as pl
from jax.experimental.pallas import tpu as pltpu
from jax.sharding import PartitionSpec as P

N = 1024
LOW = 32
SCALE = 1.0 / math.sqrt(N)
MESH = pl.DeviceIdType.MESH
BF16 = jnp.bfloat16
F32 = jnp.float32
SCALAR = 3
PIECES = (2, 2, 4)
FIRST = (0, 2, 4)
LAST = (2, 3)
ROUNDS = 7


def dot(a, b):
    return jnp.dot(a, b, preferred_element_type=F32)


def along_z(half_ref, cos_ref, sin_ref, out_ref, blocks):
    size = half_ref.shape[1]
    width = N // blocks

    @pl.loop(0, blocks)
    def _(block):
        here = pl.ds(pl.multiple_of(block * width, width), width)
        both = half_ref[...].reshape(2 * size, N)
        by_cos, by_sin = dot(both, cos_ref[:, here]), dot(both, sin_ref[:, here])
        out_ref[0, :, here] = (by_cos[:size] - by_sin[size:]).astype(BF16)
        out_ref[1, :, here] = (by_sin[:size] + by_cos[size:]).astype(BF16)


def finish(blocks, velocity_ref, scalar_ref, last_ref, cos_ref, sin_ref, velocity_out, scalar_out, result, sems):
    size = last_ref.shape[1]
    done = pl.ds(0, N // blocks - size)
    copies = [
        pltpu.make_async_copy(velocity_ref.at[0:2], velocity_out.at[0:2, :, 0], sems.at[0]),
        pltpu.make_async_copy(velocity_ref.at[2, :, done], velocity_out.at[2, :, 0, done], sems.at[1]),
        pltpu.make_async_copy(scalar_ref, scalar_out, sems.at[2]),
        pltpu.make_async_copy(result, velocity_out.at[2, :, 0, pl.ds(N // blocks - size, size)], sems.at[3]),
    ]
    for copy in copies[:3]:
        copy.start()
    along_z(last_ref, cos_ref, sin_ref, result, blocks)
    copies[3].start()
    for copy in copies:
        copy.wait()


def kernel(
    ky_count,
    kz_count,
    offsets_hbm,
    fields_ref,
    velocity_ref,
    scalar_ref,
    last_ref,
    kz_cos,
    kz_sin,
    offsets_ref,
    gathered,
    relay,
    rolled,
    back_relay,
    half_done,
    across,
    factor,
    turned,
    ky_cos,
    ky_sin,
    word,
    offsets_sem,
    relay_send,
    relay_recv,
    relay_own,
    gather_send,
    gather_recv,
    own_sem,
    kz_send,
    kz_recv,
    kz_own,
    over_send,
    over_recv,
    back_send,
    back_recv,
    back_own,
):
    ky = lax.axis_index("ky")
    kz = lax.axis_index("kz")
    rows = N // ky_count
    part = N // kz_count
    plane_count = ky_count // 2

    x, low_z, y = lax.rem(ky, 4), lax.rem(ky // 4, 2), ky // 8

    def at(new_y, new_low_z, new_x):
        return lax.rem(new_y, 4) * 8 + new_low_z * 4 + lax.rem(new_x, 4)

    partner = at(y, 1 - low_z, x)

    def each_beside_x(act):
        pl.when(x > 0)(lambda: act(at(y, low_z, x + 3)))
        pl.when(x < 3)(lambda: act(at(y, low_z, x + 1)))

    def each_beside_y(act):
        pl.when(y > 0)(lambda: act(at(y + 3, low_z, x)))
        pl.when(y < 3)(lambda: act(at(y + 1, low_z, x)))

    def count_beside(place):
        return 2 - jnp.where(place == 0, 1, 0) - jnp.where(place == 3, 1, 0)

    def kz_peers():
        return [lax.rem(kz // 2 + step // 2, 2) * 2 + lax.rem(kz + step, 2) for step in (2, 3, 1)]

    def signal(sem, **device):
        pl.semaphore_signal(sem, inc=1, device_id=device, device_id_type=MESH)

    def remote(src, dst, send_sem, recv_sem, **device):
        return pltpu.make_async_remote_copy(
            src_ref=src, dst_ref=dst, send_sem=send_sem, recv_sem=recv_sem, device_id=device, device_id_type=MESH
        )

    barrier = pltpu.get_barrier_semaphore()
    signal(barrier, ky=partner)
    each_beside_x(lambda peer: signal(barrier, ky=peer))
    each_beside_y(lambda peer: signal(barrier, ky=peer))
    for peer in kz_peers():
        signal(barrier, kz=peer)
    pl.semaphore_wait(barrier, 4 + count_beside(x) + count_beside(y))

    def send_over(field):
        for group in range(4):
            remote(
                fields_ref.at[field, :, pl.ds(group * 8 + (1 - low_z) * 4, 4)],
                relay.at[field, :, pl.ds(group * 4, 4)],
                relay_send,
                relay_recv.at[field],
                ky=partner,
            ).start()

    def all_over(field):
        return remote(relay.at[field], relay.at[field], relay_send, relay_recv.at[field], ky=partner)

    for field in (SCALAR, 0, 1, 2):
        send_over(field)

    copy_offsets = pltpu.make_async_copy(offsets_hbm, offsets_ref, offsets_sem)
    copy_offsets.start()

    for index in range(3):
        each_beside_x(lambda peer: signal(word.at[index], ky=peer))
        pl.semaphore_wait(word.at[index], count_beside(x))
    for index in range(3, 6):
        each_beside_y(lambda peer: signal(word.at[index], ky=peer))
        pl.semaphore_wait(word.at[index], count_beside(y))
    signal(word.at[6], ky=partner)
    pl.semaphore_wait(word.at[6], 1)

    def rows_of(block):
        return pl.ds(pl.multiple_of(block * rows, rows), rows)

    my_rows, partner_rows = rows_of(ky), rows_of(partner)

    def in_plane(step):
        number = lax.rem(mine + step, plane_count)
        return number, at(number // 4, low_z, number)

    mine = y * 4 + x

    def own_copy(field):
        return pltpu.make_async_copy(fields_ref.at[field, :, ky], gathered.at[field, :, my_rows], own_sem.at[field])

    def relay_copy(field):
        return pltpu.make_async_copy(
            relay.at[field, :, mine], gathered.at[field, :, partner_rows], relay_own.at[field]
        )

    def gather(field):
        own_copy(field).start()

        @pl.loop(1, plane_count)
        def _(step):
            _, peer = in_plane(step)
            remote(
                fields_ref.at[field, :, peer],
                gathered.at[field, :, my_rows],
                gather_send,
                gather_recv.at[field],
                ky=peer,
            ).start()

    def pass_on(field):
        all_over(field).wait_recv()
        relay_copy(field).start()

        @pl.loop(1, plane_count)
        def _(step):
            number, peer = in_plane(step)
            remote(
                relay.at[field, :, number],
                gathered.at[field, :, partner_rows],
                gather_send,
                gather_recv.at[field],
                ky=peer,
            ).start()

    def gather_all(field):
        others = gathered.at[field, :, pl.ds(0, (ky_count - 2) * rows)]
        return remote(others, others, gather_send, gather_recv.at[field], ky=partner)

    def wait_gathered(field):
        own_copy(field).wait()
        relay_copy(field).wait()
        gather_all(field).wait_recv()

    gather(SCALAR)
    gather(0)

    copy_offsets.wait()
    offset = offsets_ref[ky]
    some = LOW // 4

    @pl.loop(0, 4)
    def _(group):
        here = pl.ds(pl.multiple_of(group * some, some), some)
        row = group * some + lax.broadcasted_iota(jnp.int32, (some, N), 0)
        column = lax.broadcasted_iota(jnp.int32, (some, N), 1)
        low_row = group * some + lax.broadcasted_iota(jnp.int32, (some, 128), 0)

        def wave(turns):
            angle = lax.rem(turns, N).astype(F32) * (2.0 * math.pi / N)
            return jnp.cos(angle), jnp.sin(angle)

        for index, multiple, scale in ((0, LOW, SCALE), (2, 1, 1.0)):
            a, b = wave(row * multiple * column)
            a, b = a * scale, b * scale
            c, s = wave(low_row * multiple * offset)
            c, s = c[:, :1], s[:, :1]
            factor[index, here] = a
            factor[index + 1, here] = b
            turned[index, here] = a * c - b * s
            turned[index + 1, here] = a * s + b * c

    def fill(source, cos_table, sin_table):
        @pl.loop(0, N // LOW)
        def _(block):
            a = source[0, pl.ds(block, 1)]
            b = source[1, pl.ds(block, 1)]
            c, s = source[2], source[3]
            here = pl.ds(pl.multiple_of(block * LOW, LOW), LOW)
            cos_table[here] = (a * c - b * s).astype(BF16)
            sin_table[here] = (a * s + b * c).astype(BF16)

    fill(turned, ky_cos, ky_sin)

    pass_on(SCALAR)
    gather(1)
    fill(factor, kz_cos, kz_sin)
    pass_on(0)
    gather(2)

    wait_gathered(SCALAR)

    @pl.loop(0, kz_count)
    def _(block):
        here = pl.ds(pl.multiple_of(block * part, part), part)
        target = block * part + lax.broadcasted_iota(jnp.int32, (part, N), 0)
        source = lax.rem(target + (N - offset), N)
        chosen = (lax.broadcasted_iota(jnp.int32, (part, N), 1) == source).astype(F32).astype(BF16)
        for side in range(2):
            rolled[side, here] = dot(chosen, gathered[SCALAR, side]).astype(BF16)

    for group in range(4):
        remote(
            rolled.at[:, pl.ds(pl.multiple_of(group * 256 + (1 - low_z) * 128, 128), 128)],
            back_relay.at[:, pl.ds(group * 128, 128)],
            over_send,
            over_recv,
            ky=partner,
        ).start()

    own_back = pltpu.make_async_copy(rolled.at[:, my_rows], scalar_ref.at[:, ky], back_own.at[0])
    own_back.start()

    @pl.loop(1, plane_count)
    def _(step):
        _, peer = in_plane(step)
        remote(rolled.at[:, rows_of(peer)], scalar_ref.at[:, ky], back_send, back_recv, ky=peer).start()

    my_part = pl.ds(pl.multiple_of(kz * part, part), part)

    def piece_rows(field, piece):
        size = part // PIECES[field]
        return pl.ds(piece * size, size)

    def own_across(field, piece):
        some_rows = piece_rows(field, piece)
        return pltpu.make_async_copy(
            half_done.at[field, kz, :, some_rows], across.at[field, :, some_rows, my_part], kz_own.at[FIRST[field] + piece]
        )

    def all_across(field, piece):
        others = across.at[field, :, piece_rows(field, piece), pl.ds(0, N - part)]
        return remote(others, others, kz_send, kz_recv.at[FIRST[field] + piece], kz=kz_peers()[0])

    for field in range(3):
        if field:
            pass_on(field)
        wait_gathered(field)

        @pl.loop(0, kz_count)
        def _(block):
            here = pl.ds(pl.multiple_of(block * part, part), part)
            c, s = ky_cos[here], ky_sin[here]
            real, imag = gathered[field, 0], gathered[field, 1]
            half_done[field, block, 0] = (dot(c, real) - dot(s, imag)).astype(BF16)
            half_done[field, block, 1] = (dot(s, real) + dot(c, imag)).astype(BF16)

        for piece in range(PIECES[field]):
            some_rows = piece_rows(field, piece)
            for peer in kz_peers():
                remote(
                    half_done.at[field, peer, :, some_rows],
                    across.at[field, :, some_rows, my_part],
                    kz_send,
                    kz_recv.at[FIRST[field] + piece],
                    kz=peer,
                ).start()
            own_across(field, piece).start()

    over = remote(back_relay, back_relay, over_send, over_recv, ky=partner)
    over.wait_recv()
    relay_back = pltpu.make_async_copy(back_relay.at[:, rows_of(mine)], scalar_ref.at[:, partner], back_own.at[1])
    relay_back.start()

    @pl.loop(1, plane_count)
    def _(step):
        number, peer = in_plane(step)
        remote(back_relay.at[:, rows_of(number)], scalar_ref.at[:, partner], back_send, back_recv, ky=peer).start()

    for field in range(3):
        for piece in range(PIECES[field]):
            if (field, piece) == LAST:
                others_back = scalar_ref.at[:, pl.ds(0, ky_count - 2)]
                back = remote(others_back, others_back, back_send, back_recv, ky=partner)
                back.wait_recv()
                own_back.wait()
                relay_back.wait()
                remote(relay, relay, relay_send, relay_recv.at[0], ky=partner).wait_send()
                sent = gathered.at[:, :, pl.ds(0, (ky_count - 2) * rows)]
                remote(sent, sent, gather_send, gather_recv.at[0], ky=partner).wait_send()
                over.wait_send()
                back.wait_send()

            own_across(field, piece).wait()
            all_across(field, piece).wait_recv()
            if (field, piece) != LAST:
                some_rows = piece_rows(field, piece)
                along_z(
                    across.at[field, :, some_rows], kz_cos, kz_sin, velocity_ref.at[field, :, some_rows], kz_count
                )

    last_ref[...] = across[LAST[0], :, piece_rows(*LAST)]
    sent = across.at[:, :, :, pl.ds(0, N - part)]
    remote(sent, sent, kz_send, kz_recv.at[0], kz=kz_peers()[0]).wait_send()


def shards(fields, offsets):
    ky_count, kz_count = lax.axis_size("ky"), lax.axis_size("kz")
    rows, part = fields.shape[3], fields.shape[4]
    in_hbm = lambda array: pltpu.with_memory_space_constraint(array, pltpu.HBM)
    in_vmem = lambda *shape: pltpu.VMEM(shape, BF16)
    dma = lambda *shape: pltpu.SemaphoreType.DMA(shape)
    vmem, hbm = pl.BlockSpec(memory_space=pltpu.VMEM), pl.BlockSpec(memory_space=pltpu.HBM)
    shape = lambda *dims: jax.ShapeDtypeStruct(dims, BF16)
    scalar_shape = shape(2, ky_count, rows, part)
    piece = part // PIECES[LAST[0]]
    held = pl.pallas_call(
        functools.partial(kernel, ky_count, kz_count),
        out_shape=(shape(3, 2, part, N), scalar_shape, shape(2, piece, N), shape(N, N), shape(N, N)),
        in_specs=[hbm, pl.BlockSpec(memory_space=pl.ANY)],
        out_specs=(vmem,) * 5,
        scratch_shapes=[
            pltpu.SMEM((ky_count,), jnp.int32),
            in_vmem(4, 2, N, part),
            in_vmem(4, 2, ky_count // 2, rows, part),
            in_vmem(2, N, part),
            in_vmem(2, N // 2, part),
            in_vmem(3, kz_count, 2, part, part),
            in_vmem(3, 2, part, N),
            pltpu.VMEM((4, LOW, N), F32),
            pltpu.VMEM((4, LOW, N), F32),
            in_vmem(N, N),
            in_vmem(N, N),
            pltpu.SemaphoreType.REGULAR((ROUNDS,)),
            pltpu.SemaphoreType.DMA,
            pltpu.SemaphoreType.DMA,
            dma(4),
            dma(4),
            pltpu.SemaphoreType.DMA,
            dma(4),
            dma(4),
            pltpu.SemaphoreType.DMA,
            dma(sum(PIECES)),
            dma(sum(PIECES)),
            pltpu.SemaphoreType.DMA,
            pltpu.SemaphoreType.DMA,
            pltpu.SemaphoreType.DMA,
            pltpu.SemaphoreType.DMA,
            dma(2),
        ],
        compiler_params=pltpu.CompilerParams(
            collective_id=0, has_side_effects=True, vmem_limit_bytes=44 * 2**20
        ),
        name="roll_and_transform",
    )(in_hbm(offsets), in_hbm(fields))
    return pl.pallas_call(
        functools.partial(finish, kz_count),
        out_shape=(shape(3, 2, 1, part, N), scalar_shape),
        in_specs=[vmem] * 5,
        out_specs=(hbm, hbm),
        scratch_shapes=[in_vmem(2, piece, N), dma(4)],
        compiler_params=pltpu.CompilerParams(vmem_limit_bytes=8 * 2**20),
        name="finish",
    )(*held)


def solution(mesh):
    placed = (P(None, None, None, "ky", "kz"), P())
    return jax.shard_map(
        shards,
        mesh=mesh,
        in_specs=placed,
        out_specs=(P(None, None, "ky", "kz", None), P(None, None, "ky", "kz")),
        check_vma=False,
    )
```
